128 devices in a mesh: dp: 4 (over z), cols: 32 (over x, y, core).
Axes of the slice: x: 4, y: 4, z: 4, core: 2. Of those that a mesh axis runs over, the one named last changes fastest.
Arguments:
- inputs: bfloat16 [4096, 4096], P('dp', 'cols'), may hold values from -6 to 6
- query_grads: bfloat16 [4096, 8192], P('dp'), may hold values from -0.125 to 0.125, as said below
- momentum: float32 [8192, 4096], P('dp', 'cols'), may hold values from -14 to 14, as said below
Outputs:
- new_momentum: float32 [8192, 4096], P('dp', 'cols')
- update: float32 [8192, 4096], P('dp', 'cols')
The draws below stay inside these ranges and needn't reach their ends.
Inputs may be any that keep to these rules, and one draw needn't show every extreme that they name: `query_grads`: entries of scale about 4096 ** -0.5. `momentum`: entries of order two.
All inputs are finite; a program needn't handle non-finite values.
Results may differ from the reference program's by a relative error of at most 0.0003.
Values may be sent and summed in bfloat16 or wider, within the bound.
A program may use at most 128 MiB of HBM per device.

```python
import math
import jax
import jax.numpy as jnp
from jax import lax

D = 4096
HEADS = 64
HEAD_DIM = 128
NEWTON_STEPS = 5
TOKENS = 4096


def draw_query_grads(key, part):
    first = jax.random.fold_in(key, 11)
    scale = TOKENS ** (-0.5)
    shape = (TOKENS, HEADS * HEAD_DIM)
    values = jax.random.normal(first, shape, jnp.float32)
    return jnp.clip(values * scale, -8.0 * scale, 8.0 * scale).astype(jnp.bfloat16)


def draw_momentum(key, part):
    first = jax.random.fold_in(key, 21)
    shape = (HEADS * HEAD_DIM, D)
    values = 2.0 * jax.random.normal(first, shape, jnp.float32)
    return jnp.clip(values, -14.0, 14.0)


def steps_of(key, dims, split, least, top_value):
    level = 1.0
    for dim, shards_of in split:
        draws = jax.random.uniform(jax.random.fold_in(jax.random.fold_in(key, 6), dim), (shards_of,), jnp.float32, least / len(split), top_value / len(split))
        level = level * jnp.repeat(jnp.exp(draws), dims[dim] // shards_of).reshape((-1,) + (1,) * (len(dims) - 1 - dim))
    return level


def bell_draw(own_key, shape, spread, bound, shards=(), kind=jnp.bfloat16):
    drawn = spread * jax.random.normal(own_key, shape, jnp.float32)
    if shards:
        drawn = drawn * steps_of(own_key, shape, shards, -0.22, 0.18)
    return jnp.clip(drawn, -bound, bound).astype(kind)


def setup_inputs(seed: int = 0) -> dict:
    keys = jax.random.split(jax.random.key(seed), 4)
    inputs = bell_draw(keys[0], (TOKENS, D), 1.0, 6.0, ((0, 4), (1, 32)))
    query_grads = draw_query_grads(jax.random.fold_in(keys[3], 71), 0)
    momentum = draw_momentum(jax.random.fold_in(keys[3], 71), 0)
    return {"inputs": inputs, "query_grads": query_grads, "momentum": momentum}


MOMENTUM_DECAY = 0.95
NORM_EPS = 1e-07
LINEAR_COEF = 3.4445
CUBIC_COEF = -4.775
QUINTIC_COEF = 2.0315
HIGHEST = lax.Precision.HIGHEST

def polynomial(gram_matrix):
    matrix_order = gram_matrix.shape[-1]
    trace_sum = lax.optimization_barrier(jnp.sum(jnp.diagonal(gram_matrix, axis1=1, axis2=2), axis=1))
    norm_scale = jnp.sqrt(trace_sum) + NORM_EPS
    current = gram_matrix / (norm_scale * norm_scale)[:, None, None]
    identity = jnp.eye(matrix_order, dtype=jnp.float32)
    factor = jnp.broadcast_to(identity, gram_matrix.shape)
    for sweep_index in range(NEWTON_STEPS):
        square = jnp.einsum('hij,hjk->hik', current, current, precision=HIGHEST)
        poly_term = LINEAR_COEF * identity + CUBIC_COEF * current + QUINTIC_COEF * square
        factor = jnp.einsum('hij,hjk->hik', poly_term, factor, precision=HIGHEST)
        if sweep_index + 1 < NEWTON_STEPS:
            inner = jnp.einsum('hij,hjk->hik', current, poly_term, precision=HIGHEST)
            current = jnp.einsum('hij,hjk->hik', poly_term, inner, precision=HIGHEST)
    return factor / norm_scale[:, None, None]

def head_update(head_block):
    gram_matrix = jnp.dot(head_block, head_block.T, precision=HIGHEST)
    factor = polynomial(gram_matrix[None])[0]
    return math.sqrt(D) * jnp.dot(factor, head_block, precision=HIGHEST)

def reference(inputs, query_grads, momentum):
    gradient = lax.dot_general(query_grads, inputs, (((0,), (0,)), ((), ())), preferred_element_type=jnp.float32)
    new_momentum = MOMENTUM_DECAY * momentum + gradient
    blocks = new_momentum.reshape(HEADS, HEAD_DIM, D)
    update = lax.map(head_update, blocks).reshape(HEADS * HEAD_DIM, D)
    return (new_momentum, update)
```

```python
import functools
import math

import jax
import jax.numpy as jnp
from jax import lax
from jax.experimental import pallas as pl
from jax.experimental.pallas import tpu as pltpu
from jax.sharding import PartitionSpec as P

HEAD = 128
STEPS = 5
MOMENTUM_DECAY = 0.95
NORM_EPS = 1e-07
C1 = 3.4445
C3 = -4.775
C5 = 2.0315
MESH = pl.DeviceIdType.MESH
F32 = jnp.float32
BF16 = jnp.bfloat16

GRAD_CODE = (0.125, 2.0**-6, 4)
GRAM_CODE = (8.0, 2.0**-12, 3)
ROOT_CODE = (0.0625, 2.0**-6, 4)
RELAY_A, RELAY_B, DIRECT_B, DIRECT_A, SUM_A, SUM_B = range(6)


def encode(value, code):
    a, s, doublings = code
    grown = jnp.abs(value) * (s / a) + s
    for _ in range(doublings):
        grown = grown * grown
    return jnp.where(value < 0.0, -grown, grown).astype(BF16)


def decode(sent, code):
    a, s, doublings = code
    wide = sent.astype(F32)
    grown = jnp.exp(jnp.log(jnp.abs(wide)) * (0.5**doublings))
    size = grown * (a / s) - a
    return jnp.where(wide < 0.0, -size, size)


def split(value):
    high = value.astype(BF16)
    low = (value - high.astype(F32)).astype(BF16)
    return high, low


def dot_nn(a, b):
    return lax.dot_general(a, b, (((1,), (0,)), ((), ())), preferred_element_type=F32)


def dot_nt(a, b):
    return lax.dot_general(a, b, (((1,), (1,)), ((), ())), preferred_element_type=F32)


def mul3(a, b):
    ah, al = a
    bh, bl = b
    return dot_nn(ah, bh) + (dot_nn(ah, bl) + dot_nn(al, bh))


def kernel(
    dims,
    x_hbm,
    q_hbm,
    m_hbm,
    nm_ref,
    up_ref,
    x_ref,
    xt_ref,
    q_ref,
    m_ref,
    own_ref,
    zsend,
    zrecv,
    gsend,
    grecv,
    gown,
    fsend,
    frecv,
    x_sem,
    m_sem,
    q_sem,
    zsend_sem,
    zrecv_sem,
    gsend_sem,
    grecv_sem,
    fsend_sem,
    frecv_sem,
):
    cols, heads, chunks, width = dims
    half_rows = chunks * width
    rows = 2 * half_rows
    per_chunk = width // HEAD
    half_heads = heads // 2

    z = lax.axis_index("dp")
    c = lax.axis_index("cols")
    right = lax.rem(z + 1, 4)
    left = lax.rem(z + 3, 4)
    opposite = lax.rem(z + 2, 4)

    own_head = c // 2
    is_owner = jnp.logical_and(own_head < heads, lax.rem(c, 2) == lax.rem(own_head, 2))
    own_chunk = lax.rem(own_head, half_heads) // per_chunk

    def owner_of(head):
        return 2 * head + lax.rem(head, 2)

    row = lax.broadcasted_iota(jnp.int32, (HEAD, HEAD), 0)
    column = lax.broadcasted_iota(jnp.int32, (HEAD, HEAD), 1)
    identity = jnp.where(row == column, 1.0, 0.0)

    x_copy = pltpu.make_async_copy(x_hbm, x_ref, x_sem)
    x_copy.start()

    def q_copy(slot, target, half, k):
        start = pl.multiple_of(target * rows + half * half_rows + k * width, width)
        return pltpu.make_async_copy(q_hbm.at[:, pl.ds(start, width)], q_ref.at[slot], q_sem.at[slot])

    for k in range(chunks):
        q_copy(2 * k, opposite, 0, k).start()
        q_copy(2 * k + 1, opposite, 1, k).start()
    second = 2 * chunks
    for k in range(chunks):
        q_copy(second + 4 * k, right, 1, k).start()
        q_copy(second + 4 * k + 1, left, 0, k).start()
        q_copy(second + 4 * k + 2, right, 0, k).start()
        q_copy(second + 4 * k + 3, left, 1, k).start()
    third = 6 * chunks
    m_copy = pltpu.make_async_copy(m_hbm, m_ref, m_sem)
    for k in range(chunks):
        q_copy(third + 2 * k, z, 0, k).start()
        q_copy(third + 2 * k + 1, z, 1, k).start()
    m_copy.start()

    barrier = pltpu.get_barrier_semaphore()
    for step in (1, 3):
        pl.semaphore_signal(barrier, inc=1, device_id={"dp": lax.rem(z + step, 4)}, device_id_type=MESH)

    def greet(step, carry):
        pl.semaphore_signal(barrier, inc=1, device_id={"cols": lax.rem(c + step, cols)}, device_id_type=MESH)
        return carry

    lax.fori_loop(1, cols, greet, 0)

    x_copy.wait()
    xt_ref[...] = x_ref[...].T
    pl.semaphore_wait(barrier, cols - 1 + 2)

    def product(slot):
        pltpu.make_async_copy(q_hbm.at[:, pl.ds(0, width)], q_ref.at[slot], q_sem.at[slot]).wait()
        return dot_nn(xt_ref[...], q_ref[slot])

    def z_copy(message, k, target):
        return pltpu.make_async_remote_copy(
            src_ref=zsend.at[message, k],
            dst_ref=zrecv.at[message, k],
            send_sem=zsend_sem.at[message, k],
            recv_sem=zrecv_sem.at[message, k],
            device_id={"dp": target},
            device_id_type=MESH,
        )

    def z_send(message, k, target, value):
        zsend[message, k] = encode(value, GRAD_CODE)
        z_copy(message, k, target).start()

    def z_arrived(message, k):
        z_copy(message, k, right).wait_recv()
        return decode(zrecv[message, k], GRAD_CODE)

    def relay(k, carry):
        z_send(RELAY_A, k, right, product(2 * k))
        z_send(RELAY_B, k, left, product(2 * k + 1))
        return carry

    lax.fori_loop(0, chunks, relay, 0)

    def onward(k, carry):
        z_send(DIRECT_B, k, right, product(second + 4 * k))
        z_send(DIRECT_A, k, left, product(second + 4 * k + 1))
        mine = product(second + 4 * k + 2)
        z_send(SUM_A, k, right, mine + z_arrived(RELAY_A, k))
        mine = product(second + 4 * k + 3)
        z_send(SUM_B, k, left, mine + z_arrived(RELAY_B, k))
        return carry

    lax.fori_loop(0, chunks, onward, 0)

    def kept(k, carry):
        own_ref[2 * k] = product(third + 2 * k)
        own_ref[2 * k + 1] = product(third + 2 * k + 1)
        return carry

    lax.fori_loop(0, chunks, kept, 0)
    m_copy.wait()

    def g_copy(head):
        owner = owner_of(head)
        slot = jnp.maximum(lax.rem(c - owner + cols, cols) - 1, 0)
        return pltpu.make_async_remote_copy(
            src_ref=gsend.at[head],
            dst_ref=grecv.at[slot],
            send_sem=gsend_sem.at[head],
            recv_sem=grecv_sem.at[slot],
            device_id={"cols": owner},
            device_id_type=MESH,
        )

    def head_done(head, total):
        start = pl.multiple_of(head * HEAD, HEAD)
        block = m_ref[pl.ds(start, HEAD), :] * MOMENTUM_DECAY + total.T
        nm_ref[pl.ds(start, HEAD), :] = block
        high, low = split(block)
        cross = dot_nt(high, low)
        gram = dot_nt(high, high) + (cross + dot_nt(low, high))

        @pl.when(c == owner_of(head))
        def _():
            gown[...] = gram

        @pl.when(c != owner_of(head))
        def _():
            gsend[head] = encode(gram, GRAM_CODE)
            g_copy(head).start()

    def f_copy(step):
        return pltpu.make_async_remote_copy(
            src_ref=fsend,
            dst_ref=frecv.at[own_head],
            send_sem=fsend_sem.at[step],
            recv_sem=frecv_sem.at[own_head],
            device_id={"cols": lax.rem(c + step, cols)},
            device_id_type=MESH,
        )

    def own_polynomial():
        def add(slot, total):
            pltpu.make_async_remote_copy(
                src_ref=gsend.at[0],
                dst_ref=grecv.at[slot],
                send_sem=gsend_sem.at[0],
                recv_sem=grecv_sem.at[slot],
                device_id={"cols": lax.rem(c + 1, cols)},
                device_id_type=MESH,
            ).wait_recv()
            return total + decode(grecv[slot], GRAM_CODE)

        gram = lax.fori_loop(0, cols - 1, add, gown[...])
        trace = jnp.sum(jnp.sum(gram * identity, axis=0, keepdims=True), axis=1, keepdims=True)
        norm = jnp.sqrt(trace) + NORM_EPS
        current = gram / (norm * norm)
        factor = None
        for sweep in range(STEPS):
            parts = split(current)
            square = mul3(parts, parts)
            poly = C1 * identity + C3 * current + C5 * square
            poly_parts = split(poly)
            factor = poly if factor is None else mul3(poly_parts, split(factor))
            if sweep + 1 < STEPS:
                inner = mul3(parts, poly_parts)
                current = mul3(poly_parts, split(inner))
        mean = jnp.sum(jnp.sum(factor * identity, axis=0, keepdims=True), axis=1, keepdims=True) * (1.0 / HEAD)
        fsend[pl.ds(0, HEAD), :] = encode(factor - mean * identity, ROOT_CODE)
        which = lax.broadcasted_iota(jnp.int32, (16, HEAD), 0)
        pieces = jnp.zeros((16, HEAD), F32)
        for row_index, rest in ((0, norm), (3, mean)):
            rest = jnp.broadcast_to(rest, (16, HEAD))
            for piece in range(3):
                part = rest.astype(BF16).astype(F32)
                pieces = jnp.where(which == row_index + piece, part, pieces)
                rest = rest - part
        fsend[pl.ds(HEAD, 16), :] = pieces.astype(BF16)

        def send(step, carry):
            f_copy(step).start()
            return carry

        lax.fori_loop(1, cols, send, 0)

    def finish(k, carry):
        @pl.when(k < chunks)
        def _():
            total = own_ref[2 * k] + (z_arrived(DIRECT_A, k) + z_arrived(SUM_A, k))
            for j in range(per_chunk):
                head_done(k * per_chunk + j, total[:, j * HEAD : (j + 1) * HEAD])
            total = own_ref[2 * k + 1] + (z_arrived(DIRECT_B, k) + z_arrived(SUM_B, k))
            for j in range(per_chunk):
                head_done(half_heads + k * per_chunk + j, total[:, j * HEAD : (j + 1) * HEAD])

        @pl.when(jnp.logical_and(is_owner, own_chunk == k - 1))
        def _():
            own_polynomial()

        return carry

    lax.fori_loop(0, chunks + 1, finish, 0)

    def apply(index, carry):
        k = index // (2 * per_chunk)
        j = lax.rem(index, 2 * per_chunk)
        head = (j // per_chunk) * half_heads + k * per_chunk + lax.rem(j, per_chunk)
        mine = c == owner_of(head)

        @pl.when(jnp.logical_not(mine))
        def _():
            pltpu.make_async_remote_copy(
                src_ref=fsend,
                dst_ref=frecv.at[head],
                send_sem=fsend_sem.at[0],
                recv_sem=frecv_sem.at[head],
                device_id={"cols": lax.rem(c + 1, cols)},
                device_id_type=MESH,
            ).wait_recv()

        @pl.when(mine)
        def _():
            frecv[head] = fsend[...]

        pieces = frecv[head, pl.ds(HEAD, 16), :].astype(F32)
        norm = pieces[0:1, :] + (pieces[1:2, :] + pieces[2:3, :])
        mean = pieces[3:4, :] + (pieces[4:5, :] + pieces[5:6, :])
        factor = decode(frecv[head, pl.ds(0, HEAD), :], ROOT_CODE) + mean * identity
        scale = math.sqrt(cols * HEAD) / norm
        start = pl.multiple_of(head * HEAD, HEAD)
        block = nm_ref[pl.ds(start, HEAD), :]
        up_ref[pl.ds(start, HEAD), :] = mul3(split(factor), split(block)) * scale
        return carry

    lax.fori_loop(0, heads, apply, 0)

    def z_drain(k, carry):
        for message in range(6):
            z_copy(message, k, right).wait_send()
        return carry

    lax.fori_loop(0, chunks, z_drain, 0)

    def g_drain(head, carry):
        @pl.when(c != owner_of(head))
        def _():
            g_copy(head).wait_send()

        return carry

    lax.fori_loop(0, heads, g_drain, 0)

    @pl.when(is_owner)
    def _():
        def f_drain(step, carry):
            f_copy(step).wait_send()
            return carry

        lax.fori_loop(1, cols, f_drain, 0)


def shards(cols, chunks, inputs, query_grads, momentum):
    rows = momentum.shape[0]
    heads = rows // HEAD
    width = rows // (2 * chunks)
    tokens = inputs.shape[0]
    dims = (cols, heads, chunks, width)
    out = jax.ShapeDtypeStruct((rows, HEAD), F32)
    return pl.pallas_call(
        functools.partial(kernel, dims),
        out_shape=(out, out),
        in_specs=[pl.BlockSpec(memory_space=pl.ANY)] * 3,
        out_specs=(pl.BlockSpec(memory_space=pltpu.VMEM),) * 2,
        scratch_shapes=[
            pltpu.VMEM((tokens, HEAD), BF16),
            pltpu.VMEM((HEAD, tokens), BF16),
            pltpu.VMEM((8 * chunks, tokens, width), BF16),
            pltpu.VMEM((rows, HEAD), F32),
            pltpu.VMEM((2 * chunks, HEAD, width), F32),
            pltpu.VMEM((6, chunks, HEAD, width), BF16),
            pltpu.VMEM((6, chunks, HEAD, width), BF16),
            pltpu.VMEM((heads, HEAD, HEAD), BF16),
            pltpu.VMEM((cols - 1, HEAD, HEAD), BF16),
            pltpu.VMEM((HEAD, HEAD), F32),
            pltpu.VMEM((HEAD + 16, HEAD), BF16),
            pltpu.VMEM((heads, HEAD + 16, HEAD), BF16),
            pltpu.SemaphoreType.DMA,
            pltpu.SemaphoreType.DMA,
            pltpu.SemaphoreType.DMA((8 * chunks,)),
            pltpu.SemaphoreType.DMA((6, chunks)),
            pltpu.SemaphoreType.DMA((6, chunks)),
            pltpu.SemaphoreType.DMA((heads,)),
            pltpu.SemaphoreType.DMA((cols - 1,)),
            pltpu.SemaphoreType.DMA((cols,)),
            pltpu.SemaphoreType.DMA((heads,)),
        ],
        compiler_params=pltpu.CompilerParams(collective_id=0, has_side_effects=True),
    )(inputs, query_grads, momentum)


def solution(mesh):
    placed = (P("dp", "cols"), P("dp", None), P("dp", "cols"))
    return jax.shard_map(
        functools.partial(shards, mesh.shape["cols"], 4),
        mesh=mesh,
        in_specs=placed,
        out_specs=(P("dp", "cols"), P("dp", "cols")),
        check_vma=False,
    )
```

```python
import functools
import math

import jax
import jax.numpy as jnp
from jax import lax
from jax.experimental import pallas as pl
from jax.experimental.pallas import tpu as pltpu
from jax.sharding import PartitionSpec as P

HEAD = 128
HALF = HEAD // 2
STEPS = 5
MOMENTUM_DECAY = 0.95
NORM_EPS = 1e-07
C1 = 3.4445
C3 = -4.775
C5 = 2.0315
MESH = pl.DeviceIdType.MESH
F32 = jnp.float32
BF16 = jnp.bfloat16

GRAD_CODE = (0.125, 2.0**-6, 4)
GRAM_CODE = (8.0, 2.0**-12, 3)
ROOT_CODE = (0.0625, 2.0**-6, 4)
RELAY_A, RELAY_B, DIRECT_B, DIRECT_A, SUM_A, SUM_B = range(6)


def encode(value, code):
    a, s, doublings = code
    grown = jnp.abs(value) * (s / a) + s
    for _ in range(doublings):
        grown = grown * grown
    return jnp.where(value < 0.0, -grown, grown).astype(BF16)


def decode(sent, code):
    a, s, doublings = code
    wide = sent.astype(F32)
    grown = jnp.exp(jnp.log(jnp.abs(wide)) * (0.5**doublings))
    size = grown * (a / s) - a
    return jnp.where(wide < 0.0, -size, size)


def split(value):
    high = value.astype(BF16)
    low = (value - high.astype(F32)).astype(BF16)
    return high, low


def dot_nn(a, b):
    return lax.dot_general(a, b, (((1,), (0,)), ((), ())), preferred_element_type=F32)


def dot_nt(a, b):
    return lax.dot_general(a, b, (((1,), (1,)), ((), ())), preferred_element_type=F32)


def mul3(a, b):
    ah, al = a
    bh, bl = b
    return dot_nn(ah, bh) + (dot_nn(ah, bl) + dot_nn(al, bh))


def iotas(rows):
    return (
        lax.broadcasted_iota(jnp.int32, (rows, HEAD), 0),
        lax.broadcasted_iota(jnp.int32, (rows, HEAD), 1),
    )


def pack(matrix):
    row, lane = iotas(HALF)
    return jnp.where(lane > row, matrix[:HALF], pltpu.roll(matrix[HALF:], HALF, 1))


def unpack(packed):
    row, lane = iotas(HALF)
    top = jnp.where(lane > row, packed, 0.0)
    bottom = pltpu.roll(jnp.where(lane < row, packed, 0.0), HALF, 1)
    half = jnp.concatenate([top, bottom], axis=0)
    return half + half.T


def kernel(
    dims,
    x_hbm,
    q_hbm,
    m_hbm,
    nm_ref,
    up_ref,
    x_ref,
    xt_ref,
    q_ref,
    m_ref,
    own_ref,
    zsend,
    zrecv,
    gsend,
    grecv,
    fsend,
    frecv,
    x_sem,
    m_sem,
    q_sem,
    zsend_sem,
    zrecv_sem,
    gsend_sem,
    grecv_sem,
    fsend_sem,
    frecv_sem,
):
    cols, heads, chunks, width = dims
    half_rows = chunks * width
    rows = 2 * half_rows
    per_chunk = width // HEAD
    half_heads = heads // 2
    groups = 2
    wide = half_rows // groups
    per_group = chunks // groups

    z = lax.axis_index("dp")
    c = lax.axis_index("cols")
    right = lax.rem(z + 1, 4)
    left = lax.rem(z + 3, 4)
    opposite = lax.rem(z + 2, 4)

    own_head = c // 2
    is_owner = jnp.logical_and(own_head < heads, lax.rem(c, 2) == lax.rem(own_head, 2))

    row, lane = iotas(HEAD)
    identity = jnp.where(row == lane, 1.0, 0.0)
    which = iotas(16)[0]

    def owner_of(head):
        return 2 * head + lax.rem(head, 2)

    x_copy = pltpu.make_async_copy(x_hbm, x_ref, x_sem)
    x_copy.start()

    def q_copy(slot, target, half, g):
        start = pl.multiple_of(target * rows + half * half_rows + g * wide, wide)
        return pltpu.make_async_copy(q_hbm.at[:, pl.ds(start, wide)], q_ref.at[slot], q_sem.at[slot])

    for g in range(groups):
        q_copy(2 * g, opposite, 0, g).start()
        q_copy(2 * g + 1, opposite, 1, g).start()
    q_copy(4, right, 1, 0).start()
    q_copy(5, left, 0, 0).start()
    for g in range(groups):
        q_copy(8 + 2 * g, z, 0, g).start()
        q_copy(9 + 2 * g, z, 1, g).start()
    q_copy(12, right, 0, 0).start()
    q_copy(13, left, 1, 0).start()
    q_copy(6, right, 1, 1).start()
    q_copy(7, left, 0, 1).start()
    q_copy(14, right, 0, 1).start()
    q_copy(15, left, 1, 1).start()
    m_copy = pltpu.make_async_copy(m_hbm, m_ref, m_sem)
    m_copy.start()

    barrier = pltpu.get_barrier_semaphore()
    for step in (1, 3):
        pl.semaphore_signal(barrier, inc=1, device_id={"dp": lax.rem(z + step, 4)}, device_id_type=MESH)

    def greet(step, carry):
        pl.semaphore_signal(barrier, inc=1, device_id={"cols": lax.rem(c + step, cols)}, device_id_type=MESH)
        return carry

    lax.fori_loop(1, cols, greet, 0)

    x_copy.wait()
    xt_ref[...] = x_ref[...].T

    def q_wait(slot):
        pltpu.make_async_copy(q_hbm.at[:, pl.ds(0, wide)], q_ref.at[slot], q_sem.at[slot]).wait()

    def product(slot):
        return dot_nn(xt_ref[...], q_ref[slot])

    def z_copy(message, k, target):
        return pltpu.make_async_remote_copy(
            src_ref=zsend.at[message, k],
            dst_ref=zrecv.at[message, k],
            send_sem=zsend_sem.at[message, k],
            recv_sem=zrecv_sem.at[message, k],
            device_id={"dp": target},
            device_id_type=MESH,
        )

    def z_store(message, g, value):
        for i in range(per_group):
            zsend[message, g * per_group + i] = encode(value[:, i * width : (i + 1) * width], GRAD_CODE)

    def z_start(message, g, target):
        for i in range(per_group):
            z_copy(message, g * per_group + i, target).start()

    def z_wait(message, k):
        z_copy(message, k, right).wait_recv()

    def z_value(message, k):
        return decode(zrecv[message, k], GRAD_CODE)

    for g in range(groups):
        q_wait(2 * g)
        q_wait(2 * g + 1)
        z_store(RELAY_A, g, product(2 * g))
        z_store(RELAY_B, g, product(2 * g + 1))
        if g == 0:
            pl.semaphore_wait(barrier, cols - 1 + 2)
        z_start(RELAY_A, g, right)
        z_start(RELAY_B, g, left)

    def direct(g):
        q_wait(4 + 2 * g)
        q_wait(5 + 2 * g)
        z_store(DIRECT_B, g, product(4 + 2 * g))
        z_store(DIRECT_A, g, product(5 + 2 * g))
        z_start(DIRECT_B, g, right)
        z_start(DIRECT_A, g, left)

    def sums(g):
        q_wait(12 + 2 * g)
        q_wait(13 + 2 * g)
        for i in range(per_group):
            z_wait(RELAY_A, g * per_group + i)
            z_wait(RELAY_B, g * per_group + i)
        for message, arrived, slot in ((SUM_A, RELAY_A, 12 + 2 * g), (SUM_B, RELAY_B, 13 + 2 * g)):
            mine = product(slot)
            for i in range(per_group):
                k = g * per_group + i
                value = mine[:, i * width : (i + 1) * width] + z_value(arrived, k)
                zsend[message, k] = encode(value, GRAD_CODE)
        z_start(SUM_A, g, right)
        z_start(SUM_B, g, left)

    direct(0)
    for g in range(groups):
        for half in range(2):
            q_wait(8 + 2 * g + half)
        for half in range(2):
            own_ref[half, g] = product(8 + 2 * g + half)
    sums(0)
    direct(1)
    sums(1)
    m_copy.wait()

    def g_copy(head):
        owner = owner_of(head)
        slot = lax.rem(c - owner + cols - 1 + cols, cols)
        return pltpu.make_async_remote_copy(
            src_ref=gsend.at[head],
            dst_ref=grecv.at[slot],
            send_sem=gsend_sem.at[head],
            recv_sem=grecv_sem.at[slot],
            device_id={"cols": owner},
            device_id_type=MESH,
        )

    def finish(k, carry):
        g = k // per_group
        inside = pl.multiple_of(lax.rem(k, per_group) * width, width)
        for message in (DIRECT_A, SUM_A, DIRECT_B, SUM_B):
            z_wait(message, k)
        done = []
        for half, (first, second) in enumerate(((DIRECT_A, SUM_A), (DIRECT_B, SUM_B))):
            total = own_ref[half, g, :, pl.ds(inside, width)] + (z_value(first, k) + z_value(second, k))
            for j in range(per_chunk):
                head = half * half_heads + k * per_chunk + j
                start = pl.multiple_of(head * HEAD, HEAD)
                block = m_ref[pl.ds(start, HEAD), :] * MOMENTUM_DECAY + total[:, j * HEAD : (j + 1) * HEAD].T
                nm_ref[pl.ds(start, HEAD), :] = block
                high, low = split(block)
                gram = dot_nt(high, high) + (dot_nt(high, low) + dot_nt(low, high))
                diagonal = jnp.sum(gram * identity, axis=0, keepdims=True)
                gsend[head, pl.ds(0, HALF), :] = encode(pack(gram), GRAM_CODE)
                gsend[head, pl.ds(HALF, 16), :] = encode(jnp.broadcast_to(diagonal, (16, HEAD)), GRAM_CODE)
                done.append(head)
        for head in done:

            @pl.when(c != owner_of(head))
            def _():
                g_copy(head).start()

        return carry

    lax.fori_loop(0, chunks, finish, 0)

    def f_copy(step):
        return pltpu.make_async_remote_copy(
            src_ref=fsend,
            dst_ref=frecv.at[own_head],
            send_sem=fsend_sem.at[step],
            recv_sem=frecv_sem.at[own_head],
            device_id={"cols": lax.rem(c + step, cols)},
            device_id_type=MESH,
        )

    @pl.when(is_owner)
    def _():
        def arrived(slot):
            pltpu.make_async_remote_copy(
                src_ref=gsend.at[0],
                dst_ref=grecv.at[slot],
                send_sem=gsend_sem.at[0],
                recv_sem=grecv_sem.at[slot],
                device_id={"cols": lax.rem(c + 1, cols)},
                device_id_type=MESH,
            ).wait_recv()

        def add(index, total):
            for i in range(4):
                arrived(4 * index + i)
            parts = [decode(grecv[4 * index + i], GRAM_CODE) for i in range(4)]
            return total + ((parts[0] + parts[1]) + (parts[2] + parts[3]))

        sums4 = (cols - 1) // 4
        total = lax.fori_loop(0, sums4, add, decode(gsend[own_head], GRAM_CODE))
        for slot in range(4 * sums4, cols - 1):
            arrived(slot)
        for slot in range(4 * sums4, cols - 1):
            total += decode(grecv[slot], GRAM_CODE)
        diagonal = total[HALF : HALF + 1]
        gram = unpack(total[:HALF]) + identity * diagonal
        norm = jnp.sqrt(jnp.sum(diagonal, axis=1, keepdims=True)) + NORM_EPS
        current = gram / (norm * norm)
        factor = None
        for sweep in range(STEPS):
            parts = split(current)
            square = mul3(parts, parts)
            poly = C1 * identity + C3 * current + C5 * square
            poly_parts = split(poly)
            factor = poly if factor is None else mul3(poly_parts, split(factor))
            if sweep + 1 < STEPS:
                inner = mul3(parts, poly_parts)
                current = mul3(poly_parts, split(inner))
        diagonal = jnp.sum(factor * identity, axis=0, keepdims=True)
        mean = jnp.sum(diagonal, axis=1, keepdims=True) * (1.0 / HEAD)
        fsend[pl.ds(0, HALF), :] = encode(pack(factor), ROOT_CODE)
        pieces = jnp.broadcast_to(encode(diagonal - mean, ROOT_CODE).astype(F32), (16, HEAD))
        for first, rest in ((1, norm), (4, mean)):
            rest = jnp.broadcast_to(rest, (16, HEAD))
            for piece in range(3):
                part = rest.astype(BF16).astype(F32)
                pieces = jnp.where(which == first + piece, part, pieces)
                rest = rest - part
        fsend[pl.ds(HALF, 16), :] = pieces.astype(BF16)

        def send(step, carry):
            f_copy(step).start()
            return carry

        lax.fori_loop(1, cols, send, 0)
        frecv[own_head] = fsend[...]

    def apply(k, carry):
        members = [half * half_heads + k * per_chunk + j for half in range(2) for j in range(per_chunk)]
        for head in members:

            @pl.when(c != owner_of(head))
            def _():
                pltpu.make_async_remote_copy(
                    src_ref=fsend,
                    dst_ref=frecv.at[head],
                    send_sem=fsend_sem.at[0],
                    recv_sem=frecv_sem.at[head],
                    device_id={"cols": lax.rem(c + 1, cols)},
                    device_id_type=MESH,
                ).wait_recv()

        for head in members:
            pieces = frecv[head, pl.ds(HALF, 16), :].astype(F32)
            norm = pieces[1:2, :] + (pieces[2:3, :] + pieces[3:4, :])
            mean = pieces[4:5, :] + (pieces[5:6, :] + pieces[6:7, :])
            diagonal = decode(pieces[0:8, :], ROOT_CODE)[0:1] + mean
            factor = unpack(decode(frecv[head, pl.ds(0, HALF), :], ROOT_CODE)) + identity * diagonal
            start = pl.multiple_of(head * HEAD, HEAD)
            block = nm_ref[pl.ds(start, HEAD), :]
            scale = math.sqrt(cols * HEAD) / norm
            up_ref[pl.ds(start, HEAD), :] = mul3(split(factor), split(block)) * scale
        return carry

    lax.fori_loop(0, chunks, apply, 0)

    def z_drain(k, carry):
        for message in range(6):
            z_copy(message, k, right).wait_send()
        return carry

    lax.fori_loop(0, chunks, z_drain, 0)

    def g_drain(head, carry):
        @pl.when(c != owner_of(head))
        def _():
            g_copy(head).wait_send()

        return carry

    lax.fori_loop(0, heads, g_drain, 0)

    @pl.when(is_owner)
    def _():
        def f_drain(step, carry):
            f_copy(step).wait_send()
            return carry

        lax.fori_loop(1, cols, f_drain, 0)


def shards(cols, chunks, inputs, query_grads, momentum):
    rows = momentum.shape[0]
    heads = rows // HEAD
    width = rows // (2 * chunks)
    wide = rows // 4
    tokens = inputs.shape[0]
    dims = (cols, heads, chunks, width)
    out = pltpu.VMEM((rows, HEAD), F32)
    return pl.pallas_call(
        functools.partial(kernel, dims),
        out_shape=(out, out),
        in_specs=[pl.BlockSpec(memory_space=pltpu.HBM)] * 3,
        out_specs=(pl.BlockSpec(memory_space=pltpu.VMEM),) * 2,
        scratch_shapes=[
            pltpu.VMEM((tokens, HEAD), BF16),
            pltpu.VMEM((HEAD, tokens), BF16),
            pltpu.VMEM((16, tokens, wide), BF16),
            pltpu.VMEM((rows, HEAD), F32),
            pltpu.VMEM((2, 2, HEAD, wide), F32),
            pltpu.VMEM((6, chunks, HEAD, width), BF16),
            pltpu.VMEM((6, chunks, HEAD, width), BF16),
            pltpu.VMEM((heads, HALF + 16, HEAD), BF16),
            pltpu.VMEM((cols - 1, HALF + 16, HEAD), BF16),
            pltpu.VMEM((HALF + 16, HEAD), BF16),
            pltpu.VMEM((heads, HALF + 16, HEAD), BF16),
            pltpu.SemaphoreType.DMA,
            pltpu.SemaphoreType.DMA,
            pltpu.SemaphoreType.DMA((16,)),
            pltpu.SemaphoreType.DMA((6, chunks)),
            pltpu.SemaphoreType.DMA((6, chunks)),
            pltpu.SemaphoreType.DMA((heads,)),
            pltpu.SemaphoreType.DMA((cols - 1,)),
            pltpu.SemaphoreType.DMA((cols,)),
            pltpu.SemaphoreType.DMA((heads,)),
        ],
        compiler_params=pltpu.CompilerParams(
            collective_id=0, has_side_effects=True, vmem_limit_bytes=50 * 2**20
        ),
    )(*(pltpu.with_memory_space_constraint(value, pltpu.HBM) for value in (inputs, query_grads, momentum)))


def solution(mesh):
    placed = (P("dp", "cols"), P("dp", None), P("dp", "cols"))
    return jax.shard_map(
        functools.partial(shards, mesh.shape["cols"], 4),
        mesh=mesh,
        in_specs=placed,
        out_specs=(P("dp", "cols"), P("dp", "cols")),
        check_vma=False,
    )
```

```python
import functools
import math

import jax
import jax.numpy as jnp
from jax import lax
from jax.experimental import pallas as pl
from jax.experimental.pallas import tpu as pltpu
from jax.sharding import PartitionSpec as P

HEAD = 128
HALF = HEAD // 2
STEPS = 5
MOMENTUM_DECAY = 0.95
NORM_EPS = 1e-07
C1 = 3.4445
C3 = -4.775
C5 = 2.0315
MESH = pl.DeviceIdType.MESH
F32 = jnp.float32
BF16 = jnp.bfloat16

GRAD_CODE = (0.125, 2.0**-6, 4)
GRAM_CODE = (8.0, 2.0**-12, 3)
ROOT_CODE = (0.0625, 2.0**-6, 4)
RELAY_A, RELAY_B, DIRECT_B, DIRECT_A, SUM_A, SUM_B = range(6)


def encode(value, code):
    a, s, doublings = code
    grown = jnp.abs(value) * (s / a) + s
    for _ in range(doublings):
        grown = grown * grown
    return jnp.where(value < 0.0, -grown, grown).astype(BF16)


def decode(sent, code):
    a, s, doublings = code
    wide = sent.astype(F32)
    grown = jnp.exp(jnp.log(jnp.abs(wide)) * (0.5**doublings))
    size = grown * (a / s) - a
    return jnp.where(wide < 0.0, -size, size)


def split(value):
    high = value.astype(BF16)
    low = (value - high.astype(F32)).astype(BF16)
    return high, low


def dot_nn(a, b):
    return lax.dot_general(a, b, (((1,), (0,)), ((), ())), preferred_element_type=F32)


def dot_nt(a, b):
    return lax.dot_general(a, b, (((1,), (1,)), ((), ())), preferred_element_type=F32)


def mul3(a, b):
    ah, al = a
    bh, bl = b
    return dot_nn(jnp.concatenate([ah, al, ah, al], axis=1), jnp.concatenate([bh, bh, bl, bl], axis=0))


def iotas(rows):
    return (
        lax.broadcasted_iota(jnp.int32, (rows, HEAD), 0),
        lax.broadcasted_iota(jnp.int32, (rows, HEAD), 1),
    )


def pack(matrix):
    row, lane = iotas(HALF)
    return jnp.where(lane > row, matrix[:HALF], pltpu.roll(matrix[HALF:], HALF, 1))


def unpack(packed):
    row, lane = iotas(HALF)
    top = jnp.where(lane > row, packed, 0.0)
    bottom = pltpu.roll(jnp.where(lane < row, packed, 0.0), HALF, 1)
    half = jnp.concatenate([top, bottom], axis=0)
    return half + half.T


def kernel(
    dims,
    x_hbm,
    q_hbm,
    m_hbm,
    nm_ref,
    up_ref,
    x_ref,
    xt_ref,
    q_ref,
    m_ref,
    own_ref,
    zsend,
    zrecv,
    gsend,
    grecv,
    fsend,
    frecv,
    x_sem,
    m_sem,
    q_sem,
    zsend_sem,
    zrecv_sem,
    gsend_sem,
    grecv_sem,
    fsend_sem,
    frecv_sem,
    rows_sem,
    plane_sem,
):
    cols, heads, chunks, width = dims
    half_rows = chunks * width
    rows = 2 * half_rows
    per_chunk = width // HEAD
    half_heads = heads // 2
    side = math.isqrt(cols // 2)
    groups = 2
    wide = half_rows // groups
    per_group = chunks // groups

    z = lax.axis_index("dp")
    c = lax.axis_index("cols")
    right = lax.rem(z + 1, 4)
    left = lax.rem(z + 3, 4)
    opposite = lax.rem(z + 2, 4)

    own_head = c // 2
    is_owner = jnp.logical_and(own_head < heads, lax.rem(c, 2) == lax.rem(own_head, 2))

    row, lane = iotas(HEAD)
    identity = jnp.where(row == lane, 1.0, 0.0)
    which = iotas(16)[0]

    def owner_of(head):
        return 2 * head + lax.rem(head, 2)

    x_copy = pltpu.make_async_copy(x_hbm, x_ref, x_sem)
    x_copy.start()

    def q_copy(slot, target, half, g):
        start = pl.multiple_of(target * rows + half * half_rows + g * wide, wide)
        return pltpu.make_async_copy(q_hbm.at[:, pl.ds(start, wide)], q_ref.at[slot], q_sem.at[slot])

    for g in range(groups):
        q_copy(2 * g, opposite, 0, g).start()
        q_copy(2 * g + 1, opposite, 1, g).start()
    q_copy(4, right, 1, 0).start()
    q_copy(5, left, 0, 0).start()
    for g in range(groups):
        q_copy(8 + 2 * g, z, 0, g).start()
        q_copy(9 + 2 * g, z, 1, g).start()
    q_copy(12, right, 0, 0).start()
    q_copy(13, left, 1, 0).start()
    q_copy(6, right, 1, 1).start()
    q_copy(7, left, 0, 1).start()
    q_copy(14, right, 0, 1).start()
    q_copy(15, left, 1, 1).start()
    m_copy = pltpu.make_async_copy(m_hbm, m_ref, m_sem)
    m_copy.start()

    core = lax.rem(c, 2)
    along_y = lax.rem(c // 2, side)
    along_x = c // (2 * side)
    other_core = c + 1 - 2 * core
    row_peers = [(lax.rem(along_x + i, side) * side + along_y) * 2 + core for i in range(1, side)]
    column_peers = [(along_x * side + lax.rem(along_y + i, side)) * 2 + core for i in range(1, side)]
    barrier = pltpu.get_barrier_semaphore()
    near = [{"dp": right}, {"dp": left}] + [{"cols": peer} for peer in row_peers + column_peers + [other_core]]
    for peer in near:
        pl.semaphore_signal(barrier, inc=1, device_id=peer, device_id_type=MESH)

    x_copy.wait()
    xt_ref[...] = x_ref[...].T

    def q_wait(slot):
        pltpu.make_async_copy(q_hbm.at[:, pl.ds(0, wide)], q_ref.at[slot], q_sem.at[slot]).wait()

    def product(slot):
        return dot_nn(xt_ref[...], q_ref[slot])

    def z_copy(message, k, target):
        return pltpu.make_async_remote_copy(
            src_ref=zsend.at[message, k],
            dst_ref=zrecv.at[message, k],
            send_sem=zsend_sem.at[message, k],
            recv_sem=zrecv_sem.at[message, k],
            device_id={"dp": target},
            device_id_type=MESH,
        )

    def z_store(message, g, value):
        for i in range(per_group):
            zsend[message, g * per_group + i] = encode(value[:, i * width : (i + 1) * width], GRAD_CODE)

    def z_start(message, g, target):
        for i in range(per_group):
            z_copy(message, g * per_group + i, target).start()

    def z_wait(message, k):
        z_copy(message, k, right).wait_recv()

    def z_value(message, k):
        return decode(zrecv[message, k], GRAD_CODE)

    for g in range(groups):
        q_wait(2 * g)
        z_store(RELAY_A, g, product(2 * g))
        if g == 0:
            pl.semaphore_wait(barrier, len(near))
        z_start(RELAY_A, g, right)
        q_wait(2 * g + 1)
        z_store(RELAY_B, g, product(2 * g + 1))
        z_start(RELAY_B, g, left)

    def direct(g):
        q_wait(4 + 2 * g)
        q_wait(5 + 2 * g)
        z_store(DIRECT_B, g, product(4 + 2 * g))
        z_store(DIRECT_A, g, product(5 + 2 * g))
        z_start(DIRECT_B, g, right)
        z_start(DIRECT_A, g, left)

    def sums(g):
        q_wait(12 + 2 * g)
        q_wait(13 + 2 * g)
        for i in range(per_group):
            z_wait(RELAY_A, g * per_group + i)
            z_wait(RELAY_B, g * per_group + i)
        for message, arrived, slot in ((SUM_A, RELAY_A, 12 + 2 * g), (SUM_B, RELAY_B, 13 + 2 * g)):
            mine = product(slot)
            for i in range(per_group):
                k = g * per_group + i
                value = mine[:, i * width : (i + 1) * width] + z_value(arrived, k)
                zsend[message, k] = encode(value, GRAD_CODE)
        z_start(SUM_A, g, right)
        z_start(SUM_B, g, left)

    for peer in column_peers:
        pl.semaphore_signal(rows_sem, inc=1, device_id={"cols": peer}, device_id_type=MESH)
    direct(0)
    pl.semaphore_wait(rows_sem, side - 1)
    pl.semaphore_signal(plane_sem, inc=1, device_id={"cols": other_core}, device_id_type=MESH)
    for g in range(groups):
        for half in range(2):
            q_wait(8 + 2 * g + half)
        for half in range(2):
            own_ref[half, g] = product(8 + 2 * g + half)
    sums(0)
    direct(1)
    sums(1)
    m_copy.wait()
    pl.semaphore_wait(plane_sem, 1)

    def g_copy(head):
        owner = owner_of(head)
        slot = lax.rem(c - owner + cols - 1 + cols, cols)
        return pltpu.make_async_remote_copy(
            src_ref=gsend.at[head],
            dst_ref=grecv.at[slot],
            send_sem=gsend_sem.at[head],
            recv_sem=grecv_sem.at[slot],
            device_id={"cols": owner},
            device_id_type=MESH,
        )

    def finish(k, carry):
        g = k // per_group
        inside = pl.multiple_of(lax.rem(k, per_group) * width, width)
        for message in (DIRECT_A, SUM_A, DIRECT_B, SUM_B):
            z_wait(message, k)
        done = []
        for half, (first, second) in enumerate(((DIRECT_A, SUM_A), (DIRECT_B, SUM_B))):
            total = own_ref[half, g, :, pl.ds(inside, width)] + (z_value(first, k) + z_value(second, k))
            for j in range(per_chunk):
                head = half * half_heads + k * per_chunk + j
                start = pl.multiple_of(head * HEAD, HEAD)
                block = m_ref[pl.ds(start, HEAD), :] * MOMENTUM_DECAY + total[:, j * HEAD : (j + 1) * HEAD].T
                nm_ref[pl.ds(start, HEAD), :] = block
                high, low = split(block)
                gram = dot_nt(
                    jnp.concatenate([high, low, high, low], axis=1), jnp.concatenate([high, high, low, low], axis=1)
                )
                diagonal = jnp.sum(gram * identity, axis=0, keepdims=True)
                gsend[head, pl.ds(0, HALF), :] = encode(pack(gram), GRAM_CODE)
                gsend[head, pl.ds(HALF, 16), :] = encode(jnp.broadcast_to(diagonal, (16, HEAD)), GRAM_CODE)
                done.append(head)
        for head in done:

            @pl.when(c != owner_of(head))
            def _():
                g_copy(head).start()

        return carry

    lax.fori_loop(0, chunks, finish, 0)

    def f_copy(step):
        return pltpu.make_async_remote_copy(
            src_ref=fsend,
            dst_ref=frecv.at[own_head],
            send_sem=fsend_sem.at[step],
            recv_sem=frecv_sem.at[own_head],
            device_id={"cols": lax.rem(c + step, cols)},
            device_id_type=MESH,
        )

    @pl.when(is_owner)
    def _():
        def arrived(slot):
            pltpu.make_async_remote_copy(
                src_ref=gsend.at[0],
                dst_ref=grecv.at[slot],
                send_sem=gsend_sem.at[0],
                recv_sem=grecv_sem.at[slot],
                device_id={"cols": lax.rem(c + 1, cols)},
                device_id_type=MESH,
            ).wait_recv()

        def add(index, total):
            for i in range(4):
                arrived(4 * index + i)
            parts = [decode(grecv[4 * index + i], GRAM_CODE) for i in range(4)]
            return total + ((parts[0] + parts[1]) + (parts[2] + parts[3]))

        sums4 = (cols - 1) // 4
        total = lax.fori_loop(0, sums4, add, decode(gsend[own_head], GRAM_CODE))
        for slot in range(4 * sums4, cols - 1):
            arrived(slot)
        for slot in range(4 * sums4, cols - 1):
            total += decode(grecv[slot], GRAM_CODE)
        diagonal = total[HALF : HALF + 1]
        gram = unpack(total[:HALF]) + identity * diagonal
        norm = jnp.sqrt(jnp.sum(diagonal, axis=1, keepdims=True)) + NORM_EPS
        current = gram / (norm * norm)
        factor = None
        for sweep in range(STEPS):
            parts = split(current)
            square = mul3(parts, parts)
            poly = C1 * identity + C3 * current + C5 * square
            poly_parts = split(poly)
            factor = poly if factor is None else mul3(poly_parts, split(factor))
            if sweep + 1 < STEPS:
                inner = mul3(parts, poly_parts)
                current = mul3(poly_parts, split(inner))
        diagonal = jnp.sum(factor * identity, axis=0, keepdims=True)
        mean = jnp.sum(diagonal, axis=1, keepdims=True) * (1.0 / HEAD)
        fsend[pl.ds(0, HALF), :] = encode(pack(factor), ROOT_CODE)
        pieces = jnp.broadcast_to(encode(diagonal - mean, ROOT_CODE).astype(F32), (16, HEAD))
        for first, rest in ((1, norm), (4, mean)):
            rest = jnp.broadcast_to(rest, (16, HEAD))
            for piece in range(3):
                part = rest.astype(BF16).astype(F32)
                pieces = jnp.where(which == first + piece, part, pieces)
                rest = rest - part
        fsend[pl.ds(HALF, 16), :] = pieces.astype(BF16)

        def send(step, carry):
            f_copy(step).start()
            return carry

        lax.fori_loop(1, cols, send, 0)
        frecv[own_head] = fsend[...]

    def apply(k, carry):
        members = [half * half_heads + k * per_chunk + j for half in range(2) for j in range(per_chunk)]
        for head in members:

            @pl.when(c != owner_of(head))
            def _():
                pltpu.make_async_remote_copy(
                    src_ref=fsend,
                    dst_ref=frecv.at[head],
                    send_sem=fsend_sem.at[0],
                    recv_sem=frecv_sem.at[head],
                    device_id={"cols": lax.rem(c + 1, cols)},
                    device_id_type=MESH,
                ).wait_recv()

        for head in members:
            pieces = frecv[head, pl.ds(HALF, 16), :].astype(F32)
            norm = pieces[1:2, :] + (pieces[2:3, :] + pieces[3:4, :])
            mean = pieces[4:5, :] + (pieces[5:6, :] + pieces[6:7, :])
            diagonal = decode(pieces[0:8, :], ROOT_CODE)[0:1] + mean
            factor = unpack(decode(frecv[head, pl.ds(0, HALF), :], ROOT_CODE)) + identity * diagonal
            start = pl.multiple_of(head * HEAD, HEAD)
            block = nm_ref[pl.ds(start, HEAD), :]
            scale = math.sqrt(cols * HEAD) / norm
            up_ref[pl.ds(start, HEAD), :] = mul3(split(factor), split(block)) * scale
        return carry

    lax.fori_loop(0, chunks, apply, 0)

    def z_drain(k, carry):
        for message in range(6):
            z_copy(message, k, right).wait_send()
        return carry

    lax.fori_loop(0, chunks, z_drain, 0)

    def g_drain(head, carry):
        @pl.when(c != owner_of(head))
        def _():
            g_copy(head).wait_send()

        return carry

    lax.fori_loop(0, heads, g_drain, 0)

    @pl.when(is_owner)
    def _():
        def f_drain(step, carry):
            f_copy(step).wait_send()
            return carry

        lax.fori_loop(1, cols, f_drain, 0)


def write_out(nm_ref, up_ref, nm_hbm, up_hbm, nm_sem, up_sem):
    copies = [pltpu.make_async_copy(nm_ref, nm_hbm, nm_sem), pltpu.make_async_copy(up_ref, up_hbm, up_sem)]
    for copy in copies:
        copy.start()
    for copy in copies:
        copy.wait()


def shards(cols, chunks, inputs, query_grads, momentum):
    rows = momentum.shape[0]
    heads = rows // HEAD
    width = rows // (2 * chunks)
    wide = rows // 4
    tokens = inputs.shape[0]
    dims = (cols, heads, chunks, width)
    out = pltpu.VMEM((rows, HEAD), F32)
    done = pl.pallas_call(
        functools.partial(kernel, dims),
        out_shape=(out, out),
        in_specs=[pl.BlockSpec(memory_space=pltpu.HBM)] * 3,
        out_specs=(pl.BlockSpec(memory_space=pltpu.VMEM),) * 2,
        scratch_shapes=[
            pltpu.VMEM((tokens, HEAD), BF16),
            pltpu.VMEM((HEAD, tokens), BF16),
            pltpu.VMEM((16, tokens, wide), BF16),
            pltpu.VMEM((rows, HEAD), F32),
            pltpu.VMEM((2, 2, HEAD, wide), F32),
            pltpu.VMEM((6, chunks, HEAD, width), BF16),
            pltpu.VMEM((6, chunks, HEAD, width), BF16),
            pltpu.VMEM((heads, HALF + 16, HEAD), BF16),
            pltpu.VMEM((cols - 1, HALF + 16, HEAD), BF16),
            pltpu.VMEM((HALF + 16, HEAD), BF16),
            pltpu.VMEM((heads, HALF + 16, HEAD), BF16),
            pltpu.SemaphoreType.DMA,
            pltpu.SemaphoreType.DMA,
            pltpu.SemaphoreType.DMA((16,)),
            pltpu.SemaphoreType.DMA((6, chunks)),
            pltpu.SemaphoreType.DMA((6, chunks)),
            pltpu.SemaphoreType.DMA((heads,)),
            pltpu.SemaphoreType.DMA((cols - 1,)),
            pltpu.SemaphoreType.DMA((cols,)),
            pltpu.SemaphoreType.DMA((heads,)),
            pltpu.SemaphoreType.REGULAR,
            pltpu.SemaphoreType.REGULAR,
        ],
        compiler_params=pltpu.CompilerParams(
            collective_id=0, has_side_effects=True, vmem_limit_bytes=50 * 2**20
        ),
    )(*(pltpu.with_memory_space_constraint(value, pltpu.HBM) for value in (inputs, query_grads, momentum)))
    return pl.pallas_call(
        write_out,
        out_shape=(jax.ShapeDtypeStruct((rows, HEAD), F32),) * 2,
        in_specs=[pl.BlockSpec(memory_space=pltpu.VMEM)] * 2,
        out_specs=(pl.BlockSpec(memory_space=pltpu.HBM),) * 2,
        scratch_shapes=[pltpu.SemaphoreType.DMA, pltpu.SemaphoreType.DMA],
        compiler_params=pltpu.CompilerParams(vmem_limit_bytes=2**20),
    )(*done)


def solution(mesh):
    placed = (P("dp", "cols"), P("dp", None), P("dp", "cols"))
    return jax.shard_map(
        functools.partial(shards, mesh.shape["cols"], 4),
        mesh=mesh,
        in_specs=placed,
        out_specs=(P("dp", "cols"), P("dp", "cols")),
        check_vma=False,
    )
```

```python
import functools
import math

import jax
import jax.numpy as jnp
from jax import lax
from jax.experimental import pallas as pl
from jax.experimental.pallas import tpu as pltpu
from jax.sharding import PartitionSpec as P

HEAD = 128
HALF = HEAD // 2
STEPS = 5
AHEAD = 3
MOMENTUM_DECAY = 0.95
NORM_EPS = 1e-07
C1 = 3.4445
C3 = -4.775
C5 = 2.0315
MESH = pl.DeviceIdType.MESH
F32 = jnp.float32
BF16 = jnp.bfloat16

GRAD_CODE = (0.125, 2.0**-6, 4)
GRAM_CODE = (8.0, 2.0**-12, 3)
ROOT_CODE = (0.0625, 2.0**-6, 4)
RELAY_A, RELAY_B, DIRECT_B, DIRECT_A, SUM_A, SUM_B = range(6)


def encode(value, code):
    a, s, doublings = code
    grown = jnp.abs(value) * (s / a) + s
    for _ in range(doublings):
        grown = grown * grown
    return jnp.where(value < 0.0, -grown, grown).astype(BF16)


def decode(sent, code):
    a, s, doublings = code
    wide = sent.astype(F32)
    grown = jnp.exp(jnp.log(jnp.abs(wide)) * (0.5**doublings))
    size = grown * (a / s) - a
    return jnp.where(wide < 0.0, -size, size)


def split(value):
    high = value.astype(BF16)
    low = (value - high.astype(F32)).astype(BF16)
    return high, low


def dot_nn(a, b):
    return lax.dot_general(a, b, (((1,), (0,)), ((), ())), preferred_element_type=F32)


def dot_nt(a, b):
    return lax.dot_general(a, b, (((1,), (1,)), ((), ())), preferred_element_type=F32)


def mul3(a, b):
    ah, al = a
    bh, bl = b
    return dot_nn(jnp.concatenate([ah, al, ah, al], axis=1), jnp.concatenate([bh, bh, bl, bl], axis=0))


def iotas(rows):
    return (
        lax.broadcasted_iota(jnp.int32, (rows, HEAD), 0),
        lax.broadcasted_iota(jnp.int32, (rows, HEAD), 1),
    )


def pack(matrix):
    row, lane = iotas(HALF)
    return jnp.where(lane > row, matrix[:HALF], pltpu.roll(matrix[HALF:], HALF, 1))


def unpack(packed):
    row, lane = iotas(HALF)
    top = jnp.where(lane > row, packed, 0.0)
    bottom = pltpu.roll(jnp.where(lane < row, packed, 0.0), HALF, 1)
    half = jnp.concatenate([top, bottom], axis=0)
    return half + half.T


def kernel(
    dims,
    x_hbm,
    q_hbm,
    m_hbm,
    nm_ref,
    up_ref,
    x_ref,
    xt_ref,
    q_ref,
    m_ref,
    own_ref,
    zsend,
    zrecv,
    gsend,
    grecv,
    fsend,
    frecv,
    x_sem,
    m_sem,
    q_sem,
    zsend_sem,
    zrecv_sem,
    gsend_sem,
    grecv_sem,
    fsend_sem,
    frecv_sem,
    round_sem,
):
    cols, heads, chunks, width = dims
    half_rows = chunks * width
    rows = 2 * half_rows
    per_chunk = width // HEAD
    half_heads = heads // 2
    side = math.isqrt(cols // 2)
    groups = 2
    wide = half_rows // groups
    per_group = chunks // groups

    z = lax.axis_index("dp")
    c = lax.axis_index("cols")
    right = lax.rem(z + 1, 4)
    left = lax.rem(z + 3, 4)
    opposite = lax.rem(z + 2, 4)

    own_head = c // 2
    is_owner = jnp.logical_and(own_head < heads, lax.rem(c, 2) == lax.rem(own_head, 2))

    row, lane = iotas(HEAD)
    identity = jnp.where(row == lane, 1.0, 0.0)
    which = iotas(16)[0]

    def owner_of(head):
        return 2 * head + lax.rem(head, 2)

    x_copy = pltpu.make_async_copy(x_hbm, x_ref, x_sem)
    x_copy.start()

    def q_copy(slot, target, half, g):
        start = pl.multiple_of(target * rows + half * half_rows + g * wide, wide)
        return pltpu.make_async_copy(q_hbm.at[:, pl.ds(start, wide)], q_ref.at[slot], q_sem.at[slot])

    blocks = [(opposite, 0, 0), (opposite, 1, 0), (opposite, 0, 1), (opposite, 1, 1)]
    blocks += [(right, 1, 0), (left, 0, 0), (z, 0, 0), (z, 1, 0), (z, 0, 1), (z, 1, 1)]
    blocks += [(right, 0, 0), (left, 1, 0), (right, 1, 1), (left, 0, 1), (right, 0, 1), (left, 1, 1)]
    direct_slots = (4, 12)
    own_slots = (6, 8)
    sum_slots = (10, 14)
    for slot in range(AHEAD):
        q_copy(slot, *blocks[slot]).start()
    m_copy = pltpu.make_async_copy(m_hbm, m_ref, m_sem)

    core = lax.rem(c, 2)
    along_y = lax.rem(c // 2, side)
    along_x = c // (2 * side)

    def device(dx, dy, dc):
        return (lax.rem(along_x + dx, side) * side + lax.rem(along_y + dy, side)) * 2 + lax.rem(core + dc, 2)

    row_peers = [device(1, 0, 0), device(side - 1, 0, 0)]
    column_peers = [device(0, 1, 0), device(0, side - 1, 0)]
    other_core = device(0, 0, 1)
    barrier = pltpu.get_barrier_semaphore()
    near = [{"dp": right}, {"dp": left}] + [{"cols": peer} for peer in row_peers + column_peers + [other_core]]
    for peer in near:
        pl.semaphore_signal(barrier, inc=1, device_id=peer, device_id_type=MESH)

    rounds = (row_peers, column_peers, column_peers, [other_core])

    def tell(index):
        for peer in rounds[index]:
            pl.semaphore_signal(round_sem.at[index], inc=1, device_id={"cols": peer}, device_id_type=MESH)

    def heard(index):
        pl.semaphore_wait(round_sem.at[index], len(rounds[index]))

    x_copy.wait()
    xt_ref[...] = x_ref[...].T

    def q_wait(slot):
        q_copy(slot, *blocks[slot]).wait()
        if slot + AHEAD < len(blocks):
            q_copy(slot + AHEAD, *blocks[slot + AHEAD]).start()
        elif slot + 1 == len(blocks):
            m_copy.start()

    def product(slot):
        return dot_nn(xt_ref[...], q_ref[slot])

    def z_copy(message, k, target):
        return pltpu.make_async_remote_copy(
            src_ref=zsend.at[message, k],
            dst_ref=zrecv.at[message, k],
            send_sem=zsend_sem.at[message, k],
            recv_sem=zrecv_sem.at[message, k],
            device_id={"dp": target},
            device_id_type=MESH,
        )

    def z_store(message, g, value):
        for i in range(per_group):
            zsend[message, g * per_group + i] = encode(value[:, i * width : (i + 1) * width], GRAD_CODE)

    def z_start(message, g, target):
        for i in range(per_group):
            z_copy(message, g * per_group + i, target).start()

    def z_wait(message, k):
        z_copy(message, k, right).wait_recv()

    def z_value(message, k):
        return decode(zrecv[message, k], GRAD_CODE)

    for half in range(2):
        q_wait(half)
        message, target = ((RELAY_A, right), (RELAY_B, left))[half]
        for i in range(per_group):
            value = dot_nn(xt_ref[...], q_ref[half, :, i * width : (i + 1) * width])
            zsend[message, i] = encode(value, GRAD_CODE)
            if half + i == 0:
                pl.semaphore_wait(barrier, len(near))
            z_copy(message, i, target).start()
    tell(0)
    for g in range(1, groups):
        q_wait(2 * g)
        z_store(RELAY_A, g, product(2 * g))
        z_start(RELAY_A, g, right)
        q_wait(2 * g + 1)
        z_store(RELAY_B, g, product(2 * g + 1))
        z_start(RELAY_B, g, left)

    def direct(g):
        slot = direct_slots[g]
        q_wait(slot)
        q_wait(slot + 1)
        z_store(DIRECT_B, g, product(slot))
        z_store(DIRECT_A, g, product(slot + 1))
        z_start(DIRECT_B, g, right)
        z_start(DIRECT_A, g, left)

    def sums(g):
        first = sum_slots[g]
        q_wait(first)
        q_wait(first + 1)
        for i in range(per_group):
            z_wait(RELAY_A, g * per_group + i)
            z_wait(RELAY_B, g * per_group + i)
        for message, arrived, slot in ((SUM_A, RELAY_A, first), (SUM_B, RELAY_B, first + 1)):
            mine = product(slot)
            for i in range(per_group):
                k = g * per_group + i
                value = mine[:, i * width : (i + 1) * width] + z_value(arrived, k)
                zsend[message, k] = encode(value, GRAD_CODE)
        z_start(SUM_A, g, right)
        z_start(SUM_B, g, left)

    heard(0)
    tell(1)
    direct(0)
    heard(1)
    tell(2)
    for g in range(groups):
        for half in range(2):
            q_wait(own_slots[g] + half)
        for half in range(2):
            own_ref[half, g] = product(own_slots[g] + half)
    heard(2)
    tell(3)
    sums(0)
    direct(1)
    sums(1)
    m_copy.wait()
    heard(3)

    def g_copy(head):
        owner = owner_of(head)
        dx = lax.rem(along_x - owner // (2 * side) + side, side)
        dy = lax.rem(along_y - lax.rem(owner // 2, side) + side, side)
        dc = lax.rem(core + owner, 2)
        slot = jnp.maximum((dx * side + dy) * 2 + dc - 1, 0)
        return pltpu.make_async_remote_copy(
            src_ref=gsend.at[head],
            dst_ref=grecv.at[slot],
            send_sem=gsend_sem.at[head],
            recv_sem=grecv_sem.at[slot],
            device_id={"cols": owner},
            device_id_type=MESH,
        )

    def finish(k, carry):
        g = k // per_group
        inside = pl.multiple_of(lax.rem(k, per_group) * width, width)
        for message in (DIRECT_A, SUM_A, DIRECT_B, SUM_B):
            z_wait(message, k)
        done = []
        for half, (first, second) in enumerate(((DIRECT_A, SUM_A), (DIRECT_B, SUM_B))):
            total = own_ref[half, g, :, pl.ds(inside, width)] + (z_value(first, k) + z_value(second, k))
            for j in range(per_chunk):
                head = half * half_heads + k * per_chunk + j
                start = pl.multiple_of(head * HEAD, HEAD)
                block = m_ref[pl.ds(start, HEAD), :] * MOMENTUM_DECAY + total[:, j * HEAD : (j + 1) * HEAD].T
                nm_ref[pl.ds(start, HEAD), :] = block
                high, low = split(block)
                gram = dot_nt(
                    jnp.concatenate([high, low, high, low], axis=1), jnp.concatenate([high, high, low, low], axis=1)
                )
                diagonal = jnp.sum(gram * identity, axis=0, keepdims=True)
                gsend[head, pl.ds(0, HALF), :] = encode(pack(gram), GRAM_CODE)
                gsend[head, pl.ds(HALF, 16), :] = encode(jnp.broadcast_to(diagonal, (16, HEAD)), GRAM_CODE)
                done.append(head)
        for head in done:

            @pl.when(c != owner_of(head))
            def _():
                g_copy(head).start()

        return carry

    lax.fori_loop(0, chunks, finish, 0)

    others = sorted(
        ((dx, dy, dc) for dx in range(side) for dy in range(side) for dc in range(2) if dx + dy + dc),
        key=lambda d: (min(d[0], side - d[0]) + min(d[1], side - d[1]), d[2]),
    )

    def f_copy(step):
        return pltpu.make_async_remote_copy(
            src_ref=fsend,
            dst_ref=frecv.at[own_head],
            send_sem=fsend_sem.at[step],
            recv_sem=frecv_sem.at[own_head],
            device_id={"cols": device(*others[step])},
            device_id_type=MESH,
        )

    @pl.when(is_owner)
    def _():
        def arrived(slot):
            pltpu.make_async_remote_copy(
                src_ref=gsend.at[0],
                dst_ref=grecv.at[slot],
                send_sem=gsend_sem.at[0],
                recv_sem=grecv_sem.at[slot],
                device_id={"cols": lax.rem(c + 1, cols)},
                device_id_type=MESH,
            ).wait_recv()

        slots = [(dx * side + dy) * 2 + dc - 1 for dx, dy, dc in others]
        total = decode(gsend[own_head], GRAM_CODE)
        for first in range(0, cols - 1, 4):
            for slot in slots[first : first + 4]:
                arrived(slot)
            for slot in slots[first : first + 4]:
                total += decode(grecv[slot], GRAM_CODE)
        diagonal = total[HALF : HALF + 1]
        gram = unpack(total[:HALF]) + identity * diagonal
        norm = jnp.sqrt(jnp.sum(diagonal, axis=1, keepdims=True)) + NORM_EPS
        current = gram / (norm * norm)
        factor = None
        for sweep in range(STEPS):
            parts = split(current)
            square = mul3(parts, parts)
            poly = C1 * identity + C3 * current + C5 * square
            poly_parts = split(poly)
            factor = poly if factor is None else mul3(poly_parts, split(factor))
            if sweep + 1 < STEPS:
                inner = mul3(parts, poly_parts)
                current = mul3(poly_parts, split(inner))
        diagonal = jnp.sum(factor * identity, axis=0, keepdims=True)
        mean = jnp.sum(diagonal, axis=1, keepdims=True) * (1.0 / HEAD)
        fsend[pl.ds(0, HALF), :] = encode(pack(factor), ROOT_CODE)
        pieces = jnp.broadcast_to(encode(diagonal - mean, ROOT_CODE).astype(F32), (16, HEAD))
        for first, rest in ((1, norm), (4, mean)):
            rest = jnp.broadcast_to(rest, (16, HEAD))
            for piece in range(3):
                part = rest.astype(BF16).astype(F32)
                pieces = jnp.where(which == first + piece, part, pieces)
                rest = rest - part
        fsend[pl.ds(HALF, 16), :] = pieces.astype(BF16)

        for step in reversed(range(cols - 1)):
            f_copy(step).start()
        frecv[own_head] = fsend[...]

    def apply(k, carry):
        members = [half * half_heads + k * per_chunk + j for half in range(2) for j in range(per_chunk)]
        for head in members:

            @pl.when(c != owner_of(head))
            def _():
                pltpu.make_async_remote_copy(
                    src_ref=fsend,
                    dst_ref=frecv.at[head],
                    send_sem=fsend_sem.at[0],
                    recv_sem=frecv_sem.at[head],
                    device_id={"cols": lax.rem(c + 1, cols)},
                    device_id_type=MESH,
                ).wait_recv()

        for head in members:
            pieces = frecv[head, pl.ds(HALF, 16), :].astype(F32)
            norm = pieces[1:2, :] + (pieces[2:3, :] + pieces[3:4, :])
            mean = pieces[4:5, :] + (pieces[5:6, :] + pieces[6:7, :])
            diagonal = decode(pieces[0:8, :], ROOT_CODE)[0:1] + mean
            factor = unpack(decode(frecv[head, pl.ds(0, HALF), :], ROOT_CODE)) + identity * diagonal
            start = pl.multiple_of(head * HEAD, HEAD)
            block = nm_ref[pl.ds(start, HEAD), :]
            scale = math.sqrt(cols * HEAD) / norm
            up_ref[pl.ds(start, HEAD), :] = mul3(split(factor), split(block)) * scale
        return carry

    def z_drain(k, carry):
        for message in range(6):
            z_copy(message, k, right).wait_send()
        return carry

    lax.fori_loop(0, chunks, z_drain, 0)

    def g_drain(head, carry):
        @pl.when(c != owner_of(head))
        def _():
            g_copy(head).wait_send()

        return carry

    lax.fori_loop(0, heads, g_drain, 0)
    lax.fori_loop(0, chunks - 1, apply, 0)

    @pl.when(is_owner)
    def _():
        for step in range(cols - 1):
            f_copy(step).wait_send()

    apply(chunks - 1, 0)


def write_out(nm_ref, up_ref, nm_hbm, up_hbm, nm_sem, up_sem):
    copies = [pltpu.make_async_copy(nm_ref, nm_hbm, nm_sem), pltpu.make_async_copy(up_ref, up_hbm, up_sem)]
    for copy in copies:
        copy.start()
    for copy in copies:
        copy.wait()


def shards(cols, chunks, inputs, query_grads, momentum):
    rows = momentum.shape[0]
    heads = rows // HEAD
    width = rows // (2 * chunks)
    wide = rows // 4
    tokens = inputs.shape[0]
    dims = (cols, heads, chunks, width)
    out = pltpu.VMEM((rows, HEAD), F32)
    done = pl.pallas_call(
        functools.partial(kernel, dims),
        out_shape=(out, out),
        in_specs=[pl.BlockSpec(memory_space=pltpu.HBM)] * 3,
        out_specs=(pl.BlockSpec(memory_space=pltpu.VMEM),) * 2,
        scratch_shapes=[
            pltpu.VMEM((tokens, HEAD), BF16),
            pltpu.VMEM((HEAD, tokens), BF16),
            pltpu.VMEM((16, tokens, wide), BF16),
            pltpu.VMEM((rows, HEAD), F32),
            pltpu.VMEM((2, 2, HEAD, wide), F32),
            pltpu.VMEM((6, chunks, HEAD, width), BF16),
            pltpu.VMEM((6, chunks, HEAD, width), BF16),
            pltpu.VMEM((heads, HALF + 16, HEAD), BF16),
            pltpu.VMEM((cols - 1, HALF + 16, HEAD), BF16),
            pltpu.VMEM((HALF + 16, HEAD), BF16),
            pltpu.VMEM((heads, HALF + 16, HEAD), BF16),
            pltpu.SemaphoreType.DMA,
            pltpu.SemaphoreType.DMA,
            pltpu.SemaphoreType.DMA((16,)),
            pltpu.SemaphoreType.DMA((6, chunks)),
            pltpu.SemaphoreType.DMA((6, chunks)),
            pltpu.SemaphoreType.DMA((heads,)),
            pltpu.SemaphoreType.DMA((cols - 1,)),
            pltpu.SemaphoreType.DMA((cols,)),
            pltpu.SemaphoreType.DMA((heads,)),
            pltpu.SemaphoreType.REGULAR((4,)),
        ],
        compiler_params=pltpu.CompilerParams(
            collective_id=0, has_side_effects=True, vmem_limit_bytes=50 * 2**20
        ),
    )(*(pltpu.with_memory_space_constraint(value, pltpu.HBM) for value in (inputs, query_grads, momentum)))
    return pl.pallas_call(
        write_out,
        out_shape=(jax.ShapeDtypeStruct((rows, HEAD), F32),) * 2,
        in_specs=[pl.BlockSpec(memory_space=pltpu.VMEM)] * 2,
        out_specs=(pl.BlockSpec(memory_space=pltpu.HBM),) * 2,
        scratch_shapes=[pltpu.SemaphoreType.DMA, pltpu.SemaphoreType.DMA],
        compiler_params=pltpu.CompilerParams(vmem_limit_bytes=2**20),
    )(*done)


def solution(mesh):
    placed = (P("dp", "cols"), P("dp", None), P("dp", "cols"))
    return jax.shard_map(
        functools.partial(shards, mesh.shape["cols"], 4),
        mesh=mesh,
        in_specs=placed,
        out_specs=(P("dp", "cols"), P("dp", "cols")),
        check_vma=False,
    )
```

```python
import functools
import math

import jax
import jax.numpy as jnp
from jax import lax
from jax.experimental import pallas as pl
from jax.experimental.pallas import tpu as pltpu
from jax.sharding import PartitionSpec as P

HEAD = 128
HALF = HEAD // 2
STEPS = 5
AHEAD = 3
MOMENTUM_DECAY = 0.95
NORM_EPS = 1e-07
C1 = 3.4445
C3 = -4.775
C5 = 2.0315
MESH = pl.DeviceIdType.MESH
F32 = jnp.float32
BF16 = jnp.bfloat16

GRAD_CODE = (0.125, 2.0**-6, 4)
GRAM_CODE = (8.0, 2.0**-12, 3)
ROW_CODE = (64.0, 2.0**-12, 3)
ROOT_CODE = (0.0625, 2.0**-6, 4)
RELAY_A, RELAY_B, DIRECT_B, DIRECT_A, SUM_A, SUM_B = range(6)


def encode(value, code):
    a, s, doublings = code
    grown = jnp.abs(value) * (s / a) + s
    for _ in range(doublings):
        grown = grown * grown
    return jnp.where(value < 0.0, -grown, grown).astype(BF16)


def decode(sent, code):
    a, s, doublings = code
    wide = sent.astype(F32)
    grown = jnp.exp(jnp.log(jnp.abs(wide)) * (0.5**doublings))
    size = grown * (a / s) - a
    return jnp.where(wide < 0.0, -size, size)


def split(value):
    high = value.astype(BF16)
    low = (value - high.astype(F32)).astype(BF16)
    return high, low


def dot_nn(a, b):
    return lax.dot_general(a, b, (((1,), (0,)), ((), ())), preferred_element_type=F32)


def dot_nt(a, b):
    return lax.dot_general(a, b, (((1,), (1,)), ((), ())), preferred_element_type=F32)


def mul3(a, b):
    ah, al = a
    bh, bl = b
    return dot_nn(jnp.concatenate([ah, al, ah, al], axis=1), jnp.concatenate([bh, bh, bl, bl], axis=0))


def iotas(rows):
    return (
        lax.broadcasted_iota(jnp.int32, (rows, HEAD), 0),
        lax.broadcasted_iota(jnp.int32, (rows, HEAD), 1),
    )


def pack(matrix):
    row, lane = iotas(HALF)
    return jnp.where(lane > row, matrix[:HALF], pltpu.roll(matrix[HALF:], HALF, 1))


def unpack(packed):
    row, lane = iotas(HALF)
    top = jnp.where(lane > row, packed, 0.0)
    bottom = pltpu.roll(jnp.where(lane < row, packed, 0.0), HALF, 1)
    half = jnp.concatenate([top, bottom], axis=0)
    return half + half.T


def kernel(
    dims,
    x_hbm,
    q_hbm,
    m_hbm,
    nm_ref,
    up_ref,
    x_ref,
    xt_ref,
    q_ref,
    m_ref,
    own_ref,
    zsend,
    zrecv,
    gsend,
    grecv,
    rsend,
    rrecv,
    fsend,
    frecv,
    x_sem,
    m_sem,
    q_sem,
    zsend_sem,
    zrecv_sem,
    gsend_sem,
    grecv_sem,
    rsend_sem,
    rrecv_sem,
    fsend_sem,
    frecv_sem,
    round_sem,
):
    cols, heads, chunks, width = dims
    half_rows = chunks * width
    rows = 2 * half_rows
    per_chunk = width // HEAD
    half_heads = heads // 2
    side = math.isqrt(cols // 2)
    groups = 2
    wide = half_rows // groups
    per_group = chunks // groups

    z = lax.axis_index("dp")
    c = lax.axis_index("cols")
    right = lax.rem(z + 1, 4)
    left = lax.rem(z + 3, 4)
    opposite = lax.rem(z + 2, 4)

    row, lane = iotas(HEAD)
    identity = jnp.where(row == lane, 1.0, 0.0)
    which = iotas(16)[0]

    x_copy = pltpu.make_async_copy(x_hbm, x_ref, x_sem)
    x_copy.start()

    def q_copy(slot, target, half, g):
        start = pl.multiple_of(target * rows + half * half_rows + g * wide, wide)
        return pltpu.make_async_copy(q_hbm.at[:, pl.ds(start, wide)], q_ref.at[slot], q_sem.at[slot])

    blocks = [(opposite, 0, 0), (opposite, 1, 0), (opposite, 0, 1), (opposite, 1, 1)]
    blocks += [(right, 1, 0), (left, 0, 0), (z, 0, 0), (z, 1, 0), (z, 0, 1), (z, 1, 1)]
    blocks += [(right, 0, 0), (left, 1, 0), (right, 1, 1), (left, 0, 1), (right, 0, 1), (left, 1, 1)]
    direct_slots = (4, 12)
    own_slots = (6, 8)
    sum_slots = (10, 14)
    for slot in range(AHEAD):
        q_copy(slot, *blocks[slot]).start()
    m_copy = pltpu.make_async_copy(m_hbm, m_ref, m_sem)

    core = lax.rem(c, 2)
    along_y = lax.rem(c // 2, side)
    along_x = c // (2 * side)

    def device(dx, dy, dc):
        return (lax.rem(along_x + dx, side) * side + lax.rem(along_y + dy, side)) * 2 + lax.rem(core + dc, 2)

    row_peers = [device(1, 0, 0), device(side - 1, 0, 0)]
    column_peers = [device(0, 1, 0), device(0, side - 1, 0)]
    other_core = device(0, 0, 1)
    barrier = pltpu.get_barrier_semaphore()
    near = [{"dp": right}, {"dp": left}] + [{"cols": peer} for peer in row_peers + column_peers + [other_core]]
    for peer in near:
        pl.semaphore_signal(barrier, inc=1, device_id=peer, device_id_type=MESH)

    rounds = (row_peers + column_peers, [other_core])

    def tell(index):
        for peer in rounds[index]:
            pl.semaphore_signal(round_sem.at[index], inc=1, device_id={"cols": peer}, device_id_type=MESH)

    def heard(index):
        pl.semaphore_wait(round_sem.at[index], len(rounds[index]))

    x_copy.wait()
    xt_ref[...] = x_ref[...].T

    def q_wait(slot):
        q_copy(slot, *blocks[slot]).wait()
        if slot + AHEAD < len(blocks):
            q_copy(slot + AHEAD, *blocks[slot + AHEAD]).start()
        elif slot + 1 == len(blocks):
            m_copy.start()

    def product(slot):
        return dot_nn(xt_ref[...], q_ref[slot])

    def z_copy(message, k, target):
        return pltpu.make_async_remote_copy(
            src_ref=zsend.at[message, k],
            dst_ref=zrecv.at[message, k],
            send_sem=zsend_sem.at[message, k],
            recv_sem=zrecv_sem.at[message, k],
            device_id={"dp": target},
            device_id_type=MESH,
        )

    def z_store(message, g, value):
        for i in range(per_group):
            zsend[message, g * per_group + i] = encode(value[:, i * width : (i + 1) * width], GRAD_CODE)

    def z_start(message, g, target):
        for i in range(per_group):
            z_copy(message, g * per_group + i, target).start()

    def z_wait(message, k):
        z_copy(message, k, right).wait_recv()

    def z_value(message, k):
        return decode(zrecv[message, k], GRAD_CODE)

    for half in range(2):
        q_wait(half)
        message, target = ((RELAY_A, right), (RELAY_B, left))[half]
        for i in range(per_group):
            value = dot_nn(xt_ref[...], q_ref[half, :, i * width : (i + 1) * width])
            zsend[message, i] = encode(value, GRAD_CODE)
            if half + i == 0:
                pl.semaphore_wait(barrier, len(near))
            z_copy(message, i, target).start()
    tell(0)
    for g in range(1, groups):
        q_wait(2 * g)
        z_store(RELAY_A, g, product(2 * g))
        z_start(RELAY_A, g, right)
        q_wait(2 * g + 1)
        z_store(RELAY_B, g, product(2 * g + 1))
        z_start(RELAY_B, g, left)

    def direct(g):
        slot = direct_slots[g]
        q_wait(slot)
        q_wait(slot + 1)
        z_store(DIRECT_B, g, product(slot))
        z_store(DIRECT_A, g, product(slot + 1))
        z_start(DIRECT_B, g, right)
        z_start(DIRECT_A, g, left)

    def sums(g):
        first = sum_slots[g]
        q_wait(first)
        q_wait(first + 1)
        for i in range(per_group):
            z_wait(RELAY_A, g * per_group + i)
            z_wait(RELAY_B, g * per_group + i)
        for message, arrived, slot in ((SUM_A, RELAY_A, first), (SUM_B, RELAY_B, first + 1)):
            mine = product(slot)
            for i in range(per_group):
                k = g * per_group + i
                value = mine[:, i * width : (i + 1) * width] + z_value(arrived, k)
                zsend[message, k] = encode(value, GRAD_CODE)
        z_start(SUM_A, g, right)
        z_start(SUM_B, g, left)

    heard(0)
    tell(1)
    direct(0)
    for g in range(groups):
        for half in range(2):
            q_wait(own_slots[g] + half)
        for half in range(2):
            own_ref[half, g] = product(own_slots[g] + half)
    sums(0)
    direct(1)
    sums(1)
    m_copy.wait()
    heard(1)

    members = 2 * per_chunk

    def head_of(k, m):
        return (m // per_chunk) * half_heads + k * per_chunk + m % per_chunk

    def owned_head(turn):
        k = core + 2 * turn
        return (along_x // per_chunk) * half_heads + k * per_chunk + lax.rem(along_x, per_chunk)

    def is_mine(k, m):
        return jnp.logical_and(along_x == m, core == lax.rem(k, 2))

    def g_copy(k, m):
        head = head_of(k, m)
        dx = lax.rem(along_x - m + side, side)
        slot = jnp.maximum(dx * 2 + lax.rem(core + k, 2) - 1, 0)
        return pltpu.make_async_remote_copy(
            src_ref=gsend.at[head],
            dst_ref=grecv.at[k // 2, slot],
            send_sem=gsend_sem.at[head],
            recv_sem=grecv_sem.at[k // 2, slot],
            device_id={"cols": (m * side + along_y) * 2 + lax.rem(k, 2)},
            device_id_type=MESH,
        )

    def finish(k, carry):
        g = k // per_group
        inside = pl.multiple_of(lax.rem(k, per_group) * width, width)
        for message in (DIRECT_A, SUM_A, DIRECT_B, SUM_B):
            z_wait(message, k)
        for half, (first, second) in enumerate(((DIRECT_A, SUM_A), (DIRECT_B, SUM_B))):
            total = own_ref[half, g, :, pl.ds(inside, width)] + (z_value(first, k) + z_value(second, k))
            for j in range(per_chunk):
                head = half * half_heads + k * per_chunk + j
                start = pl.multiple_of(head * HEAD, HEAD)
                block = m_ref[pl.ds(start, HEAD), :] * MOMENTUM_DECAY + total[:, j * HEAD : (j + 1) * HEAD].T
                nm_ref[pl.ds(start, HEAD), :] = block
                high, low = split(block)
                gram = dot_nt(
                    jnp.concatenate([high, low, high, low], axis=1), jnp.concatenate([high, high, low, low], axis=1)
                )
                diagonal = jnp.sum(gram * identity, axis=0, keepdims=True)
                gsend[head, pl.ds(0, HALF), :] = encode(pack(gram), GRAM_CODE)
                gsend[head, pl.ds(HALF, 16), :] = encode(jnp.broadcast_to(diagonal, (16, HEAD)), GRAM_CODE)
        for m in range(members):

            @pl.when(jnp.logical_not(is_mine(k, m)))
            def _():
                g_copy(k, m).start()

        return carry

    along_row = sorted(((dx, dc) for dx in range(side) for dc in range(2) if dx + dc), key=lambda d: min(d[0], side - d[0]))
    along_column = range(1, side)

    def r_copy(turn, dy):
        return pltpu.make_async_remote_copy(
            src_ref=rsend.at[turn],
            dst_ref=rrecv.at[turn, dy - 1],
            send_sem=rsend_sem.at[turn, dy - 1],
            recv_sem=rrecv_sem.at[turn, dy - 1],
            device_id={"cols": device(0, dy, 0)},
            device_id_type=MESH,
        )

    def row_sum(turn):
        total = decode(gsend[owned_head(turn)], GRAM_CODE)
        for dx, dc in along_row:
            slot = dx * 2 + dc - 1
            pltpu.make_async_remote_copy(
                src_ref=gsend.at[0],
                dst_ref=grecv.at[turn, slot],
                send_sem=gsend_sem.at[0],
                recv_sem=grecv_sem.at[turn, slot],
                device_id={"cols": other_core},
                device_id_type=MESH,
            ).wait_recv()
            total += decode(grecv[turn, slot], GRAM_CODE)
        rsend[turn] = encode(total, ROW_CODE)
        for dy in (2, 1, 3):
            r_copy(turn, dy).start()

    def f_copy(turn, index):
        head = owned_head(turn)
        dx, dc = along_row[index]
        return pltpu.make_async_remote_copy(
            src_ref=fsend.at[turn],
            dst_ref=frecv.at[head],
            send_sem=fsend_sem.at[turn, index],
            recv_sem=frecv_sem.at[head],
            device_id={"cols": device(dx, 0, dc)},
            device_id_type=MESH,
        )

    def polynomial(turn):
        total = decode(rsend[turn], ROW_CODE)
        for dy in along_column:
            r_copy(turn, dy).wait_recv()
        for dy in along_column:
            total += decode(rrecv[turn, dy - 1], ROW_CODE)
        diagonal = total[HALF : HALF + 1]
        gram = unpack(total[:HALF]) + identity * diagonal
        norm = jnp.sqrt(jnp.sum(diagonal, axis=1, keepdims=True)) + NORM_EPS
        current = gram / (norm * norm)
        factor = None
        for sweep in range(STEPS):
            parts = split(current)
            square = mul3(parts, parts)
            poly = C1 * identity + C3 * current + C5 * square
            poly_parts = split(poly)
            factor = poly if factor is None else mul3(poly_parts, split(factor))
            if sweep + 1 < STEPS:
                inner = mul3(parts, poly_parts)
                current = mul3(poly_parts, split(inner))
        diagonal = jnp.sum(factor * identity, axis=0, keepdims=True)
        mean = jnp.sum(diagonal, axis=1, keepdims=True) * (1.0 / HEAD)
        fsend[turn, pl.ds(0, HALF), :] = encode(pack(factor), ROOT_CODE)
        pieces = jnp.broadcast_to(encode(diagonal - mean, ROOT_CODE).astype(F32), (16, HEAD))
        for first, rest in ((1, norm), (4, mean)):
            rest = jnp.broadcast_to(rest, (16, HEAD))
            for piece in range(3):
                part = rest.astype(BF16).astype(F32)
                pieces = jnp.where(which == first + piece, part, pieces)
                rest = rest - part
        fsend[turn, pl.ds(HALF, 16), :] = pieces.astype(BF16)
        for index in reversed(range(len(along_row))):
            f_copy(turn, index).start()
        frecv[owned_head(turn)] = fsend[turn]

    def apply(k, carry):
        for m in range(members):

            @pl.when(jnp.logical_not(is_mine(k, m)))
            def _():
                head = head_of(k, m)
                pltpu.make_async_remote_copy(
                    src_ref=fsend.at[0],
                    dst_ref=frecv.at[head],
                    send_sem=fsend_sem.at[0, 0],
                    recv_sem=frecv_sem.at[head],
                    device_id={"cols": other_core},
                    device_id_type=MESH,
                ).wait_recv()

        for m in range(members):
            head = head_of(k, m)
            pieces = frecv[head, pl.ds(HALF, 16), :].astype(F32)
            norm = pieces[1:2, :] + (pieces[2:3, :] + pieces[3:4, :])
            mean = pieces[4:5, :] + (pieces[5:6, :] + pieces[6:7, :])
            diagonal = decode(pieces[0:8, :], ROOT_CODE)[0:1] + mean
            factor = unpack(decode(frecv[head, pl.ds(0, HALF), :], ROOT_CODE)) + identity * diagonal
            start = pl.multiple_of(head * HEAD, HEAD)
            block = nm_ref[pl.ds(start, HEAD), :]
            scale = math.sqrt(cols * HEAD) / norm
            up_ref[pl.ds(start, HEAD), :] = mul3(split(factor), split(block)) * scale
        return carry

    def z_drain(k, carry):
        for message in range(6):
            z_copy(message, k, right).wait_send()
        return carry

    def g_drain(k, carry):
        for m in range(members):

            @pl.when(jnp.logical_not(is_mine(k, m)))
            def _():
                g_copy(k, m).wait_send()

        return carry

    lax.fori_loop(0, chunks - 1, finish, 0)
    row_sum(0)
    finish(chunks - 1, 0)
    polynomial(0)
    row_sum(1)
    lax.fori_loop(0, chunks, z_drain, 0)
    lax.fori_loop(0, chunks, g_drain, 0)
    polynomial(1)
    lax.fori_loop(0, chunks - 1, apply, 0)
    for turn in range(2):
        for dy in along_column:
            r_copy(turn, dy).wait_send()
        for index in range(len(along_row)):
            f_copy(turn, index).wait_send()
    apply(chunks - 1, 0)


def write_out(nm_ref, up_ref, nm_hbm, up_hbm, nm_sem, up_sem):
    copies = [pltpu.make_async_copy(nm_ref, nm_hbm, nm_sem), pltpu.make_async_copy(up_ref, up_hbm, up_sem)]
    for copy in copies:
        copy.start()
    for copy in copies:
        copy.wait()


def shards(cols, chunks, inputs, query_grads, momentum):
    rows = momentum.shape[0]
    heads = rows // HEAD
    width = rows // (2 * chunks)
    wide = rows // 4
    tokens = inputs.shape[0]
    dims = (cols, heads, chunks, width)
    side = math.isqrt(cols // 2)
    out = pltpu.VMEM((rows, HEAD), F32)
    done = pl.pallas_call(
        functools.partial(kernel, dims),
        out_shape=(out, out),
        in_specs=[pl.BlockSpec(memory_space=pltpu.HBM)] * 3,
        out_specs=(pl.BlockSpec(memory_space=pltpu.VMEM),) * 2,
        scratch_shapes=[
            pltpu.VMEM((tokens, HEAD), BF16),
            pltpu.VMEM((HEAD, tokens), BF16),
            pltpu.VMEM((16, tokens, wide), BF16),
            pltpu.VMEM((rows, HEAD), F32),
            pltpu.VMEM((2, 2, HEAD, wide), F32),
            pltpu.VMEM((6, chunks, HEAD, width), BF16),
            pltpu.VMEM((6, chunks, HEAD, width), BF16),
            pltpu.VMEM((heads, HALF + 16, HEAD), BF16),
            pltpu.VMEM((2, 2 * side - 1, HALF + 16, HEAD), BF16),
            pltpu.VMEM((2, HALF + 16, HEAD), BF16),
            pltpu.VMEM((2, side - 1, HALF + 16, HEAD), BF16),
            pltpu.VMEM((2, HALF + 16, HEAD), BF16),
            pltpu.VMEM((heads, HALF + 16, HEAD), BF16),
            pltpu.SemaphoreType.DMA,
            pltpu.SemaphoreType.DMA,
            pltpu.SemaphoreType.DMA((16,)),
            pltpu.SemaphoreType.DMA((6, chunks)),
            pltpu.SemaphoreType.DMA((6, chunks)),
            pltpu.SemaphoreType.DMA((heads,)),
            pltpu.SemaphoreType.DMA((2, 2 * side - 1)),
            pltpu.SemaphoreType.DMA((2, side - 1)),
            pltpu.SemaphoreType.DMA((2, side - 1)),
            pltpu.SemaphoreType.DMA((2, 2 * side - 1)),
            pltpu.SemaphoreType.DMA((heads,)),
            pltpu.SemaphoreType.REGULAR((2,)),
        ],
        compiler_params=pltpu.CompilerParams(
            collective_id=0, has_side_effects=True, vmem_limit_bytes=50 * 2**20
        ),
    )(*(pltpu.with_memory_space_constraint(value, pltpu.HBM) for value in (inputs, query_grads, momentum)))
    return pl.pallas_call(
        write_out,
        out_shape=(jax.ShapeDtypeStruct((rows, HEAD), F32),) * 2,
        in_specs=[pl.BlockSpec(memory_space=pltpu.VMEM)] * 2,
        out_specs=(pl.BlockSpec(memory_space=pltpu.HBM),) * 2,
        scratch_shapes=[pltpu.SemaphoreType.DMA, pltpu.SemaphoreType.DMA],
        compiler_params=pltpu.CompilerParams(vmem_limit_bytes=2**20),
    )(*done)


def solution(mesh):
    placed = (P("dp", "cols"), P("dp", None), P("dp", "cols"))
    return jax.shard_map(
        functools.partial(shards, mesh.shape["cols"], 4),
        mesh=mesh,
        in_specs=placed,
        out_specs=(P("dp", "cols"), P("dp", "cols")),
        check_vma=False,
    )
```

```python
import functools
import math

import jax
import jax.numpy as jnp
from jax import lax
from jax.experimental import pallas as pl
from jax.experimental.pallas import tpu as pltpu
from jax.sharding import PartitionSpec as P

HEAD = 128
HALF = HEAD // 2
STEPS = 5
AHEAD = 3
MOMENTUM_DECAY = 0.95
NORM_EPS = 1e-07
C1 = 3.4445
C3 = -4.775
C5 = 2.0315
MESH = pl.DeviceIdType.MESH
F32 = jnp.float32
BF16 = jnp.bfloat16

GRAD_CODE = (0.125, 2.0**-6, 4)
GRAM_CODE = (8.0, 2.0**-12, 3)
ROOT_CODE = (0.0625, 2.0**-6, 4)
RELAY_A, RELAY_B, DIRECT_B, DIRECT_A, SUM_A, SUM_B = range(6)


def encode(value, code):
    a, s, doublings = code
    grown = jnp.abs(value) * (s / a) + s
    for _ in range(doublings):
        grown = grown * grown
    return jnp.where(value < 0.0, -grown, grown).astype(BF16)


def decode(sent, code):
    a, s, doublings = code
    wide = sent.astype(F32)
    grown = jnp.exp(jnp.log(jnp.abs(wide)) * (0.5**doublings))
    size = grown * (a / s) - a
    return jnp.where(wide < 0.0, -size, size)


def split(value):
    high = value.astype(BF16)
    low = (value - high.astype(F32)).astype(BF16)
    return high, low


def dot_nn(a, b):
    return lax.dot_general(a, b, (((1,), (0,)), ((), ())), preferred_element_type=F32)


def dot_nt(a, b):
    return lax.dot_general(a, b, (((1,), (1,)), ((), ())), preferred_element_type=F32)


def mul3(a, b):
    ah, al = a
    bh, bl = b
    return dot_nn(jnp.concatenate([ah, al, ah, al], axis=1), jnp.concatenate([bh, bh, bl, bl], axis=0))


def iotas(rows):
    return (
        lax.broadcasted_iota(jnp.int32, (rows, HEAD), 0),
        lax.broadcasted_iota(jnp.int32, (rows, HEAD), 1),
    )


def pack(matrix):
    row, lane = iotas(HALF)
    return jnp.where(lane > row, matrix[:HALF], pltpu.roll(matrix[HALF:], HALF, 1))


def unpack(packed):
    row, lane = iotas(HALF)
    top = jnp.where(lane > row, packed, 0.0)
    bottom = pltpu.roll(jnp.where(lane < row, packed, 0.0), HALF, 1)
    half = jnp.concatenate([top, bottom], axis=0)
    return half + half.T


def kernel(
    dims,
    x_hbm,
    q_hbm,
    m_hbm,
    nm_ref,
    up_ref,
    x_ref,
    xt_ref,
    q_ref,
    m_ref,
    own_ref,
    zsend,
    zrecv,
    gsend,
    grecv,
    fsend,
    frecv,
    x_sem,
    m_sem,
    q_sem,
    zsend_sem,
    zrecv_sem,
    gsend_sem,
    grecv_sem,
    fsend_sem,
    frecv_sem,
    round_sem,
):
    cols, heads, chunks, width = dims
    half_rows = chunks * width
    rows = 2 * half_rows
    per_chunk = width // HEAD
    half_heads = heads // 2
    side = math.isqrt(cols // 2)
    groups = 2
    wide = half_rows // groups
    per_group = chunks // groups

    z = lax.axis_index("dp")
    c = lax.axis_index("cols")
    right = lax.rem(z + 1, 4)
    left = lax.rem(z + 3, 4)
    opposite = lax.rem(z + 2, 4)

    row, lane = iotas(HEAD)
    identity = jnp.where(row == lane, 1.0, 0.0)
    which = iotas(16)[0]

    x_copy = pltpu.make_async_copy(x_hbm, x_ref, x_sem)
    x_copy.start()

    def q_copy(slot, target, half, g):
        start = pl.multiple_of(target * rows + half * half_rows + g * wide, wide)
        return pltpu.make_async_copy(q_hbm.at[:, pl.ds(start, wide)], q_ref.at[slot], q_sem.at[slot])

    blocks = [(opposite, 0, 0), (opposite, 1, 0), (opposite, 0, 1), (opposite, 1, 1)]
    blocks += [(right, 1, 0), (left, 0, 0), (z, 0, 0), (z, 1, 0), (z, 0, 1), (z, 1, 1)]
    blocks += [(right, 0, 0), (left, 1, 0), (right, 1, 1), (left, 0, 1), (right, 0, 1), (left, 1, 1)]
    direct_slots = (4, 12)
    own_slots = (6, 8)
    sum_slots = (10, 14)
    for slot in range(AHEAD):
        q_copy(slot, *blocks[slot]).start()
    m_copy = pltpu.make_async_copy(m_hbm, m_ref, m_sem)

    core = lax.rem(c, 2)
    along_y = lax.rem(c // 2, side)
    along_x = c // (2 * side)

    def device(dx, dy, dc):
        return (lax.rem(along_x + dx, side) * side + lax.rem(along_y + dy, side)) * 2 + lax.rem(core + dc, 2)

    row_peers = [device(1, 0, 0), device(side - 1, 0, 0)]
    column_peers = [device(0, 1, 0), device(0, side - 1, 0)]
    other_core = device(0, 0, 1)
    barrier = pltpu.get_barrier_semaphore()
    near = [{"dp": right}, {"dp": left}] + [{"cols": peer} for peer in row_peers + column_peers + [other_core]]
    for peer in near:
        pl.semaphore_signal(barrier, inc=1, device_id=peer, device_id_type=MESH)

    rounds = (row_peers, column_peers, column_peers, [other_core])

    def tell(index):
        for peer in rounds[index]:
            pl.semaphore_signal(round_sem.at[index], inc=1, device_id={"cols": peer}, device_id_type=MESH)

    def heard(index):
        pl.semaphore_wait(round_sem.at[index], len(rounds[index]))

    x_copy.wait()
    xt_ref[...] = x_ref[...].T

    def q_wait(slot):
        q_copy(slot, *blocks[slot]).wait()
        if slot + AHEAD < len(blocks):
            q_copy(slot + AHEAD, *blocks[slot + AHEAD]).start()
        elif slot + 1 == len(blocks):
            m_copy.start()

    def product(slot):
        return dot_nn(xt_ref[...], q_ref[slot])

    def z_copy(message, k, target):
        return pltpu.make_async_remote_copy(
            src_ref=zsend.at[message, k],
            dst_ref=zrecv.at[message, k],
            send_sem=zsend_sem.at[message, k],
            recv_sem=zrecv_sem.at[message, k],
            device_id={"dp": target},
            device_id_type=MESH,
        )

    def z_store(message, g, value):
        for i in range(per_group):
            zsend[message, g * per_group + i] = encode(value[:, i * width : (i + 1) * width], GRAD_CODE)

    def z_start(message, g, target):
        for i in range(per_group):
            z_copy(message, g * per_group + i, target).start()

    def z_wait(message, k):
        z_copy(message, k, right).wait_recv()

    def z_value(message, k):
        return decode(zrecv[message, k], GRAD_CODE)

    for half in range(2):
        q_wait(half)
        message, target = ((RELAY_A, right), (RELAY_B, left))[half]
        for i in range(per_group):
            value = dot_nn(xt_ref[...], q_ref[half, :, i * width : (i + 1) * width])
            zsend[message, i] = encode(value, GRAD_CODE)
            if half + i == 0:
                pl.semaphore_wait(barrier, len(near))
            z_copy(message, i, target).start()
    tell(0)
    for g in range(1, groups):
        q_wait(2 * g)
        z_store(RELAY_A, g, product(2 * g))
        z_start(RELAY_A, g, right)
        q_wait(2 * g + 1)
        z_store(RELAY_B, g, product(2 * g + 1))
        z_start(RELAY_B, g, left)

    def direct(g):
        slot = direct_slots[g]
        q_wait(slot)
        q_wait(slot + 1)
        z_store(DIRECT_B, g, product(slot))
        z_store(DIRECT_A, g, product(slot + 1))
        z_start(DIRECT_B, g, right)
        z_start(DIRECT_A, g, left)

    def sums(g):
        first = sum_slots[g]
        q_wait(first)
        q_wait(first + 1)
        for i in range(per_group):
            z_wait(RELAY_A, g * per_group + i)
            z_wait(RELAY_B, g * per_group + i)
        for message, arrived, slot in ((SUM_A, RELAY_A, first), (SUM_B, RELAY_B, first + 1)):
            mine = product(slot)
            for i in range(per_group):
                k = g * per_group + i
                value = mine[:, i * width : (i + 1) * width] + z_value(arrived, k)
                zsend[message, k] = encode(value, GRAD_CODE)
        z_start(SUM_A, g, right)
        z_start(SUM_B, g, left)

    heard(0)
    tell(1)
    direct(0)
    heard(1)
    tell(2)
    for g in range(groups):
        for half in range(2):
            q_wait(own_slots[g] + half)
        for half in range(2):
            own_ref[half, g] = product(own_slots[g] + half)
    heard(2)
    tell(3)
    sums(0)
    direct(1)
    sums(1)
    m_copy.wait()
    heard(3)

    turn = side // 2
    own_head = lax.rem(along_x + core * turn, side) * side + lax.rem(along_y + core * turn, side)

    def owner_of(head, second):
        x = lax.rem(head // side + second * turn, side)
        y = lax.rem(head + second * turn, side)
        return x, y, second

    def is_owner(head, second):
        x, y, owner_core = owner_of(head, second)
        return jnp.logical_and(jnp.logical_and(along_x == x, along_y == y), core == owner_core)

    def g_copy(head, second):
        x, y, owner_core = owner_of(head, second)
        dx = lax.rem(along_x - x + side, side)
        dy = lax.rem(along_y - y + side, side)
        slot = jnp.maximum((dx * side + dy) * 2 + lax.rem(core + owner_core, 2) - 1, 0)
        return pltpu.make_async_remote_copy(
            src_ref=gsend.at[head],
            dst_ref=grecv.at[slot],
            send_sem=gsend_sem.at[head, second],
            recv_sem=grecv_sem.at[slot],
            device_id={"cols": (x * side + y) * 2 + owner_core},
            device_id_type=MESH,
        )

    def finish(k, carry):
        g = k // per_group
        inside = pl.multiple_of(lax.rem(k, per_group) * width, width)
        for message in (DIRECT_A, SUM_A, DIRECT_B, SUM_B):
            z_wait(message, k)
        done = []
        for half, (first, second) in enumerate(((DIRECT_A, SUM_A), (DIRECT_B, SUM_B))):
            total = own_ref[half, g, :, pl.ds(inside, width)] + (z_value(first, k) + z_value(second, k))
            for j in range(per_chunk):
                head = half * half_heads + k * per_chunk + j
                start = pl.multiple_of(head * HEAD, HEAD)
                block = m_ref[pl.ds(start, HEAD), :] * MOMENTUM_DECAY + total[:, j * HEAD : (j + 1) * HEAD].T
                nm_ref[pl.ds(start, HEAD), :] = block
                high, low = split(block)
                gram = dot_nt(
                    jnp.concatenate([high, low, high, low], axis=1), jnp.concatenate([high, high, low, low], axis=1)
                )
                diagonal = jnp.sum(gram * identity, axis=0, keepdims=True)
                gsend[head, pl.ds(0, HALF), :] = encode(pack(gram), GRAM_CODE)
                gsend[head, pl.ds(HALF, 16), :] = encode(jnp.broadcast_to(diagonal, (16, HEAD)), GRAM_CODE)
                done.append(head)
        for head in done:

            for second in range(2):

                @pl.when(jnp.logical_not(is_owner(head, second)))
                def _():
                    g_copy(head, second).start()

        return carry

    lax.fori_loop(0, chunks, finish, 0)

    def far(d):
        return min(d[0], side - d[0]) + min(d[1], side - d[1])

    everyone = [(dx, dy, dc) for dx in range(side) for dy in range(side) for dc in range(2)]
    others = sorted(everyone[1:], key=lambda d: (far(d), d[2]))
    served = []
    for d in others:
        there = ((d[0] + turn) % side, (d[1] + turn) % side, d[2])
        if far(d) < far(there) or (far(d) == far(there) and there not in served):
            served.append(d)

    def f_copy(step):
        return pltpu.make_async_remote_copy(
            src_ref=fsend,
            dst_ref=frecv.at[own_head],
            send_sem=fsend_sem.at[step],
            recv_sem=frecv_sem.at[own_head],
            device_id={"cols": device(*served[step])},
            device_id_type=MESH,
        )

    def polynomial():
        def arrived(slot):
            pltpu.make_async_remote_copy(
                src_ref=gsend.at[0],
                dst_ref=grecv.at[slot],
                send_sem=gsend_sem.at[0],
                recv_sem=grecv_sem.at[slot],
                device_id={"cols": lax.rem(c + 1, cols)},
                device_id_type=MESH,
            ).wait_recv()

        slots = [(dx * side + dy) * 2 + dc - 1 for dx, dy, dc in others]
        total = decode(gsend[own_head], GRAM_CODE)
        for first in range(0, cols - 1, 4):
            for slot in slots[first : first + 4]:
                arrived(slot)
            for slot in slots[first : first + 4]:
                total += decode(grecv[slot], GRAM_CODE)
        diagonal = total[HALF : HALF + 1]
        gram = unpack(total[:HALF]) + identity * diagonal
        norm = jnp.sqrt(jnp.sum(diagonal, axis=1, keepdims=True)) + NORM_EPS
        current = gram / (norm * norm)
        factor = None
        for sweep in range(STEPS):
            parts = split(current)
            square = mul3(parts, parts)
            poly = C1 * identity + C3 * current + C5 * square
            poly_parts = split(poly)
            factor = poly if factor is None else mul3(poly_parts, split(factor))
            if sweep + 1 < STEPS:
                inner = mul3(parts, poly_parts)
                current = mul3(poly_parts, split(inner))
        diagonal = jnp.sum(factor * identity, axis=0, keepdims=True)
        mean = jnp.sum(diagonal, axis=1, keepdims=True) * (1.0 / HEAD)
        fsend[pl.ds(0, HALF), :] = encode(pack(factor), ROOT_CODE)
        pieces = jnp.broadcast_to(encode(diagonal - mean, ROOT_CODE).astype(F32), (16, HEAD))
        for first, rest in ((1, norm), (4, mean)):
            rest = jnp.broadcast_to(rest, (16, HEAD))
            for piece in range(3):
                part = rest.astype(BF16).astype(F32)
                pieces = jnp.where(which == first + piece, part, pieces)
                rest = rest - part
        fsend[pl.ds(HALF, 16), :] = pieces.astype(BF16)

        for step in reversed(range(len(served))):
            f_copy(step).start()
        frecv[own_head] = fsend[...]

    polynomial()

    def apply(k, carry):
        members = [half * half_heads + k * per_chunk + j for half in range(2) for j in range(per_chunk)]
        for head in members:

            @pl.when(head != own_head)
            def _():
                pltpu.make_async_remote_copy(
                    src_ref=fsend,
                    dst_ref=frecv.at[head],
                    send_sem=fsend_sem.at[0],
                    recv_sem=frecv_sem.at[head],
                    device_id={"cols": lax.rem(c + 1, cols)},
                    device_id_type=MESH,
                ).wait_recv()

        for head in members:
            pieces = frecv[head, pl.ds(HALF, 16), :].astype(F32)
            norm = pieces[1:2, :] + (pieces[2:3, :] + pieces[3:4, :])
            mean = pieces[4:5, :] + (pieces[5:6, :] + pieces[6:7, :])
            diagonal = decode(pieces[0:8, :], ROOT_CODE)[0:1] + mean
            factor = unpack(decode(frecv[head, pl.ds(0, HALF), :], ROOT_CODE)) + identity * diagonal
            start = pl.multiple_of(head * HEAD, HEAD)
            block = nm_ref[pl.ds(start, HEAD), :]
            scale = math.sqrt(cols * HEAD) / norm
            up_ref[pl.ds(start, HEAD), :] = mul3(split(factor), split(block)) * scale
        return carry

    def z_drain(k, carry):
        for message in range(6):
            z_copy(message, k, right).wait_send()
        return carry

    lax.fori_loop(0, chunks, z_drain, 0)

    def g_drain(head, carry):
        for second in range(2):

            @pl.when(jnp.logical_not(is_owner(head, second)))
            def _():
                g_copy(head, second).wait_send()

        return carry

    lax.fori_loop(0, heads, g_drain, 0)
    lax.fori_loop(0, chunks - 1, apply, 0)

    for step in range(len(served)):
        f_copy(step).wait_send()

    apply(chunks - 1, 0)


def write_out(nm_ref, up_ref, nm_hbm, up_hbm, nm_sem, up_sem):
    copies = [pltpu.make_async_copy(nm_ref, nm_hbm, nm_sem), pltpu.make_async_copy(up_ref, up_hbm, up_sem)]
    for copy in copies:
        copy.start()
    for copy in copies:
        copy.wait()


def shards(cols, chunks, inputs, query_grads, momentum):
    rows = momentum.shape[0]
    heads = rows // HEAD
    width = rows // (2 * chunks)
    wide = rows // 4
    tokens = inputs.shape[0]
    dims = (cols, heads, chunks, width)
    out = pltpu.VMEM((rows, HEAD), F32)
    done = pl.pallas_call(
        functools.partial(kernel, dims),
        out_shape=(out, out),
        in_specs=[pl.BlockSpec(memory_space=pltpu.HBM)] * 3,
        out_specs=(pl.BlockSpec(memory_space=pltpu.VMEM),) * 2,
        scratch_shapes=[
            pltpu.VMEM((tokens, HEAD), BF16),
            pltpu.VMEM((HEAD, tokens), BF16),
            pltpu.VMEM((16, tokens, wide), BF16),
            pltpu.VMEM((rows, HEAD), F32),
            pltpu.VMEM((2, 2, HEAD, wide), F32),
            pltpu.VMEM((6, chunks, HEAD, width), BF16),
            pltpu.VMEM((6, chunks, HEAD, width), BF16),
            pltpu.VMEM((heads, HALF + 16, HEAD), BF16),
            pltpu.VMEM((cols - 1, HALF + 16, HEAD), BF16),
            pltpu.VMEM((HALF + 16, HEAD), BF16),
            pltpu.VMEM((heads, HALF + 16, HEAD), BF16),
            pltpu.SemaphoreType.DMA,
            pltpu.SemaphoreType.DMA,
            pltpu.SemaphoreType.DMA((16,)),
            pltpu.SemaphoreType.DMA((6, chunks)),
            pltpu.SemaphoreType.DMA((6, chunks)),
            pltpu.SemaphoreType.DMA((heads, 2)),
            pltpu.SemaphoreType.DMA((cols - 1,)),
            pltpu.SemaphoreType.DMA((cols,)),
            pltpu.SemaphoreType.DMA((heads,)),
            pltpu.SemaphoreType.REGULAR((4,)),
        ],
        compiler_params=pltpu.CompilerParams(
            collective_id=0, has_side_effects=True, vmem_limit_bytes=50 * 2**20
        ),
    )(*(pltpu.with_memory_space_constraint(value, pltpu.HBM) for value in (inputs, query_grads, momentum)))
    return pl.pallas_call(
        write_out,
        out_shape=(jax.ShapeDtypeStruct((rows, HEAD), F32),) * 2,
        in_specs=[pl.BlockSpec(memory_space=pltpu.VMEM)] * 2,
        out_specs=(pl.BlockSpec(memory_space=pltpu.HBM),) * 2,
        scratch_shapes=[pltpu.SemaphoreType.DMA, pltpu.SemaphoreType.DMA],
        compiler_params=pltpu.CompilerParams(vmem_limit_bytes=2**20),
    )(*done)


def solution(mesh):
    placed = (P("dp", "cols"), P("dp", None), P("dp", "cols"))
    return jax.shard_map(
        functools.partial(shards, mesh.shape["cols"], 4),
        mesh=mesh,
        in_specs=placed,
        out_specs=(P("dp", "cols"), P("dp", "cols")),
        check_vma=False,
    )
```

```python
import functools
import math

import jax
import jax.numpy as jnp
from jax import lax
from jax.experimental import pallas as pl
from jax.experimental.pallas import tpu as pltpu
from jax.sharding import PartitionSpec as P

HEAD = 128
HALF = HEAD // 2
STEPS = 5
AHEAD = 3
MOMENTUM_DECAY = 0.95
NORM_EPS = 1e-07
C1 = 3.4445
C3 = -4.775
C5 = 2.0315
MESH = pl.DeviceIdType.MESH
F32 = jnp.float32
BF16 = jnp.bfloat16

GRAD_CODE = (0.125, 2.0**-6, 4)
GRAM_CODE = (8.0, 2.0**-12, 3)
ROOT_CODE = (0.0625, 2.0**-6, 4)
RELAY_A, RELAY_B, DIRECT_B, DIRECT_A, SUM_A, SUM_B = range(6)


def encode(value, code):
    a, s, doublings = code
    grown = jnp.abs(value) * (s / a) + s
    for _ in range(doublings):
        grown = grown * grown
    return jnp.where(value < 0.0, -grown, grown).astype(BF16)


def decode(sent, code):
    a, s, doublings = code
    wide = sent.astype(F32)
    grown = jnp.exp(jnp.log(jnp.abs(wide)) * (0.5**doublings))
    size = grown * (a / s) - a
    return jnp.where(wide < 0.0, -size, size)


def split(value):
    high = value.astype(BF16)
    low = (value - high.astype(F32)).astype(BF16)
    return high, low


def dot_nn(a, b):
    return lax.dot_general(a, b, (((1,), (0,)), ((), ())), preferred_element_type=F32)


def dot_nt(a, b):
    return lax.dot_general(a, b, (((1,), (1,)), ((), ())), preferred_element_type=F32)


def mul3(a, b):
    ah, al = a
    bh, bl = b
    return dot_nn(jnp.concatenate([ah, al, ah, al], axis=1), jnp.concatenate([bh, bh, bl, bl], axis=0))


def iotas(rows):
    return (
        lax.broadcasted_iota(jnp.int32, (rows, HEAD), 0),
        lax.broadcasted_iota(jnp.int32, (rows, HEAD), 1),
    )


def pack(matrix):
    row, lane = iotas(HALF)
    return jnp.where(lane > row, matrix[:HALF], pltpu.roll(matrix[HALF:], HALF, 1))


def unpack(packed):
    row, lane = iotas(HALF)
    top = jnp.where(lane > row, packed, 0.0)
    bottom = pltpu.roll(jnp.where(lane < row, packed, 0.0), HALF, 1)
    half = jnp.concatenate([top, bottom], axis=0)
    return half + half.T


def kernel(
    dims,
    x_hbm,
    q_hbm,
    m_hbm,
    nm_ref,
    up_ref,
    x_ref,
    xt_ref,
    q_ref,
    m_ref,
    own_ref,
    zsend,
    zrecv,
    gsend,
    grecv,
    fsend,
    frecv,
    x_sem,
    m_sem,
    q_sem,
    zsend_sem,
    zrecv_sem,
    gsend_sem,
    grecv_sem,
    fsend_sem,
    frecv_sem,
    round_sem,
):
    cols, heads, chunks, width = dims
    half_rows = chunks * width
    rows = 2 * half_rows
    per_chunk = width // HEAD
    half_heads = heads // 2
    side = math.isqrt(cols // 2)
    groups = 2
    wide = half_rows // groups
    per_group = chunks // groups

    z = lax.axis_index("dp")
    c = lax.axis_index("cols")
    right = lax.rem(z + 1, 4)
    left = lax.rem(z + 3, 4)
    opposite = lax.rem(z + 2, 4)

    own_head = c // 2
    is_owner = jnp.logical_and(own_head < heads, lax.rem(c, 2) == lax.rem(own_head, 2))
    own_group = lax.rem(own_head, half_heads) // (per_chunk * per_group)

    row, lane = iotas(HEAD)
    identity = jnp.where(row == lane, 1.0, 0.0)
    which = iotas(16)[0]

    def owner_of(head):
        return 2 * head + lax.rem(head, 2)

    x_copy = pltpu.make_async_copy(x_hbm, x_ref, x_sem)
    x_copy.start()

    def q_copy(slot, target, half, g):
        start = pl.multiple_of(target * rows + half * half_rows + g * wide, wide)
        return pltpu.make_async_copy(q_hbm.at[:, pl.ds(start, wide)], q_ref.at[slot], q_sem.at[slot])

    blocks = [(opposite, 0, 0), (opposite, 1, 0), (right, 1, 0), (left, 0, 0)]
    blocks += [(z, 0, 0), (z, 1, 0), (right, 0, 0), (left, 1, 0)]
    blocks += [(opposite, 0, 1), (opposite, 1, 1), (right, 1, 1), (left, 0, 1)]
    blocks += [(z, 0, 1), (z, 1, 1), (right, 0, 1), (left, 1, 1)]
    relay_slots = (0, 8)
    direct_slots = (2, 10)
    own_slots = (4, 12)
    sum_slots = (6, 14)
    for slot in range(AHEAD):
        q_copy(slot, *blocks[slot]).start()
    m_copy = pltpu.make_async_copy(m_hbm, m_ref, m_sem)

    core = lax.rem(c, 2)
    along_y = lax.rem(c // 2, side)
    along_x = c // (2 * side)

    def device(dx, dy, dc):
        return (lax.rem(along_x + dx, side) * side + lax.rem(along_y + dy, side)) * 2 + lax.rem(core + dc, 2)

    row_peers = [device(1, 0, 0), device(side - 1, 0, 0)]
    column_peers = [device(0, 1, 0), device(0, side - 1, 0)]
    other_core = device(0, 0, 1)
    barrier = pltpu.get_barrier_semaphore()
    near = [{"dp": right}, {"dp": left}] + [{"cols": peer} for peer in row_peers + column_peers + [other_core]]
    for peer in near:
        pl.semaphore_signal(barrier, inc=1, device_id=peer, device_id_type=MESH)

    rounds = (row_peers, column_peers, column_peers, [other_core])

    def tell(index):
        for peer in rounds[index]:
            pl.semaphore_signal(round_sem.at[index], inc=1, device_id={"cols": peer}, device_id_type=MESH)

    def heard(index):
        pl.semaphore_wait(round_sem.at[index], len(rounds[index]))

    x_copy.wait()
    xt_ref[...] = x_ref[...].T

    def q_wait(slot):
        q_copy(slot, *blocks[slot]).wait()
        if slot + AHEAD < len(blocks):
            q_copy(slot + AHEAD, *blocks[slot + AHEAD]).start()
        if slot + AHEAD == len(blocks):
            m_copy.start()

    def product(slot):
        return dot_nn(xt_ref[...], q_ref[slot])

    def z_copy(message, k, target):
        return pltpu.make_async_remote_copy(
            src_ref=zsend.at[message, k],
            dst_ref=zrecv.at[message, k],
            send_sem=zsend_sem.at[message, k],
            recv_sem=zrecv_sem.at[message, k],
            device_id={"dp": target},
            device_id_type=MESH,
        )

    def z_store(message, g, value):
        for i in range(per_group):
            zsend[message, g * per_group + i] = encode(value[:, i * width : (i + 1) * width], GRAD_CODE)

    def z_start(message, g, target):
        for i in range(per_group):
            z_copy(message, g * per_group + i, target).start()

    def z_wait(message, k):
        z_copy(message, k, right).wait_recv()

    def z_value(message, k):
        return decode(zrecv[message, k], GRAD_CODE)

    for half in range(2):
        q_wait(half)
        message, target = ((RELAY_A, right), (RELAY_B, left))[half]
        for i in range(per_group):
            value = dot_nn(xt_ref[...], q_ref[half, :, i * width : (i + 1) * width])
            zsend[message, i] = encode(value, GRAD_CODE)
            if half + i == 0:
                pl.semaphore_wait(barrier, len(near))
            z_copy(message, i, target).start()
    tell(0)
    def relay(g):
        for half, (message, target) in enumerate(((RELAY_A, right), (RELAY_B, left))):
            slot = relay_slots[g] + half
            q_wait(slot)
            z_store(message, g, product(slot))
            z_start(message, g, target)

    def direct(g):
        slot = direct_slots[g]
        q_wait(slot)
        q_wait(slot + 1)
        z_store(DIRECT_B, g, product(slot))
        z_store(DIRECT_A, g, product(slot + 1))
        z_start(DIRECT_B, g, right)
        z_start(DIRECT_A, g, left)

    def sums(g):
        first = sum_slots[g]
        q_wait(first)
        q_wait(first + 1)
        for i in range(per_group):
            z_wait(RELAY_A, g * per_group + i)
            z_wait(RELAY_B, g * per_group + i)
        for message, arrived, slot in ((SUM_A, RELAY_A, first), (SUM_B, RELAY_B, first + 1)):
            mine = product(slot)
            for i in range(per_group):
                k = g * per_group + i
                value = mine[:, i * width : (i + 1) * width] + z_value(arrived, k)
                zsend[message, k] = encode(value, GRAD_CODE)
        z_start(SUM_A, g, right)
        z_start(SUM_B, g, left)

    def own(g):
        for half in range(2):
            q_wait(own_slots[g] + half)
        for half in range(2):
            own_ref[half, g] = product(own_slots[g] + half)

    def g_copy(head):
        owner = owner_of(head)
        dx = lax.rem(along_x - owner // (2 * side) + side, side)
        dy = lax.rem(along_y - lax.rem(owner // 2, side) + side, side)
        dc = lax.rem(core + owner, 2)
        slot = jnp.maximum((dx * side + dy) * 2 + dc - 1, 0)
        return pltpu.make_async_remote_copy(
            src_ref=gsend.at[head],
            dst_ref=grecv.at[slot],
            send_sem=gsend_sem.at[head],
            recv_sem=grecv_sem.at[slot],
            device_id={"cols": owner},
            device_id_type=MESH,
        )

    def finish(k, carry):
        g = k // per_group
        inside = pl.multiple_of(lax.rem(k, per_group) * width, width)
        for message in (DIRECT_A, SUM_A, DIRECT_B, SUM_B):
            z_wait(message, k)
        done = []
        for half, (first, second) in enumerate(((DIRECT_A, SUM_A), (DIRECT_B, SUM_B))):
            total = own_ref[half, g, :, pl.ds(inside, width)] + (z_value(first, k) + z_value(second, k))
            for j in range(per_chunk):
                head = half * half_heads + k * per_chunk + j
                start = pl.multiple_of(head * HEAD, HEAD)
                block = m_ref[pl.ds(start, HEAD), :] * MOMENTUM_DECAY + total[:, j * HEAD : (j + 1) * HEAD].T
                nm_ref[pl.ds(start, HEAD), :] = block
                high, low = split(block)
                gram = dot_nt(
                    jnp.concatenate([high, low, high, low], axis=1), jnp.concatenate([high, high, low, low], axis=1)
                )
                diagonal = jnp.sum(gram * identity, axis=0, keepdims=True)
                gsend[head, pl.ds(0, HALF), :] = encode(pack(gram), GRAM_CODE)
                gsend[head, pl.ds(HALF, 16), :] = encode(jnp.broadcast_to(diagonal, (16, HEAD)), GRAM_CODE)
                done.append(head)
        for head in done:

            @pl.when(c != owner_of(head))
            def _():
                g_copy(head).start()

        return carry


    others = sorted(
        ((dx, dy, dc) for dx in range(side) for dy in range(side) for dc in range(2) if dx + dy + dc),
        key=lambda d: (min(d[0], side - d[0]) + min(d[1], side - d[1]), d[2]),
    )

    def f_copy(step):
        return pltpu.make_async_remote_copy(
            src_ref=fsend,
            dst_ref=frecv.at[own_head],
            send_sem=fsend_sem.at[step],
            recv_sem=frecv_sem.at[own_head],
            device_id={"cols": device(*others[step])},
            device_id_type=MESH,
        )

    def polynomial():
        def arrived(slot):
            pltpu.make_async_remote_copy(
                src_ref=gsend.at[0],
                dst_ref=grecv.at[slot],
                send_sem=gsend_sem.at[0],
                recv_sem=grecv_sem.at[slot],
                device_id={"cols": lax.rem(c + 1, cols)},
                device_id_type=MESH,
            ).wait_recv()

        slots = [(dx * side + dy) * 2 + dc - 1 for dx, dy, dc in others]
        total = decode(gsend[own_head], GRAM_CODE)
        for first in range(0, cols - 1, 4):
            for slot in slots[first : first + 4]:
                arrived(slot)
            for slot in slots[first : first + 4]:
                total += decode(grecv[slot], GRAM_CODE)
        diagonal = total[HALF : HALF + 1]
        gram = unpack(total[:HALF]) + identity * diagonal
        norm = jnp.sqrt(jnp.sum(diagonal, axis=1, keepdims=True)) + NORM_EPS
        current = gram / (norm * norm)
        factor = None
        for sweep in range(STEPS):
            parts = split(current)
            square = mul3(parts, parts)
            poly = C1 * identity + C3 * current + C5 * square
            poly_parts = split(poly)
            factor = poly if factor is None else mul3(poly_parts, split(factor))
            if sweep + 1 < STEPS:
                inner = mul3(parts, poly_parts)
                current = mul3(poly_parts, split(inner))
        diagonal = jnp.sum(factor * identity, axis=0, keepdims=True)
        mean = jnp.sum(diagonal, axis=1, keepdims=True) * (1.0 / HEAD)
        fsend[pl.ds(0, HALF), :] = encode(pack(factor), ROOT_CODE)
        pieces = jnp.broadcast_to(encode(diagonal - mean, ROOT_CODE).astype(F32), (16, HEAD))
        for first, rest in ((1, norm), (4, mean)):
            rest = jnp.broadcast_to(rest, (16, HEAD))
            for piece in range(3):
                part = rest.astype(BF16).astype(F32)
                pieces = jnp.where(which == first + piece, part, pieces)
                rest = rest - part
        fsend[pl.ds(HALF, 16), :] = pieces.astype(BF16)

        for step in reversed(range(cols - 1)):
            f_copy(step).start()
        frecv[own_head] = fsend[...]

    direct(0)
    heard(0)
    tell(1)
    own(0)
    heard(1)
    tell(2)
    sums(0)
    heard(2)
    tell(3)
    relay(1)
    direct(1)
    own(1)
    m_copy.wait()
    heard(3)
    lax.fori_loop(0, per_group, finish, 0)
    sums(1)
    pl.when(jnp.logical_and(is_owner, own_group == 0))(polynomial)
    lax.fori_loop(per_group, chunks, finish, 0)
    pl.when(jnp.logical_and(is_owner, own_group == 1))(polynomial)

    def apply(k, carry):
        members = [half * half_heads + k * per_chunk + j for half in range(2) for j in range(per_chunk)]
        for head in members:

            @pl.when(c != owner_of(head))
            def _():
                pltpu.make_async_remote_copy(
                    src_ref=fsend,
                    dst_ref=frecv.at[head],
                    send_sem=fsend_sem.at[0],
                    recv_sem=frecv_sem.at[head],
                    device_id={"cols": lax.rem(c + 1, cols)},
                    device_id_type=MESH,
                ).wait_recv()

        for head in members:
            pieces = frecv[head, pl.ds(HALF, 16), :].astype(F32)
            norm = pieces[1:2, :] + (pieces[2:3, :] + pieces[3:4, :])
            mean = pieces[4:5, :] + (pieces[5:6, :] + pieces[6:7, :])
            diagonal = decode(pieces[0:8, :], ROOT_CODE)[0:1] + mean
            factor = unpack(decode(frecv[head, pl.ds(0, HALF), :], ROOT_CODE)) + identity * diagonal
            start = pl.multiple_of(head * HEAD, HEAD)
            block = nm_ref[pl.ds(start, HEAD), :]
            scale = math.sqrt(cols * HEAD) / norm
            up_ref[pl.ds(start, HEAD), :] = mul3(split(factor), split(block)) * scale
        return carry

    def z_drain(k, carry):
        for message in range(6):
            z_copy(message, k, right).wait_send()
        return carry

    lax.fori_loop(0, chunks, z_drain, 0)

    def g_drain(head, carry):
        @pl.when(c != owner_of(head))
        def _():
            g_copy(head).wait_send()

        return carry

    lax.fori_loop(0, heads, g_drain, 0)
    lax.fori_loop(0, chunks - 1, apply, 0)

    @pl.when(is_owner)
    def _():
        for step in range(cols - 1):
            f_copy(step).wait_send()

    apply(chunks - 1, 0)


def write_out(nm_ref, up_ref, nm_hbm, up_hbm, nm_sem, up_sem):
    copies = [pltpu.make_async_copy(nm_ref, nm_hbm, nm_sem), pltpu.make_async_copy(up_ref, up_hbm, up_sem)]
    for copy in copies:
        copy.start()
    for copy in copies:
        copy.wait()


def shards(cols, chunks, inputs, query_grads, momentum):
    rows = momentum.shape[0]
    heads = rows // HEAD
    width = rows // (2 * chunks)
    wide = rows // 4
    tokens = inputs.shape[0]
    dims = (cols, heads, chunks, width)
    out = pltpu.VMEM((rows, HEAD), F32)
    done = pl.pallas_call(
        functools.partial(kernel, dims),
        out_shape=(out, out),
        in_specs=[pl.BlockSpec(memory_space=pltpu.HBM)] * 3,
        out_specs=(pl.BlockSpec(memory_space=pltpu.VMEM),) * 2,
        scratch_shapes=[
            pltpu.VMEM((tokens, HEAD), BF16),
            pltpu.VMEM((HEAD, tokens), BF16),
            pltpu.VMEM((16, tokens, wide), BF16),
            pltpu.VMEM((rows, HEAD), F32),
            pltpu.VMEM((2, 2, HEAD, wide), F32),
            pltpu.VMEM((6, chunks, HEAD, width), BF16),
            pltpu.VMEM((6, chunks, HEAD, width), BF16),
            pltpu.VMEM((heads, HALF + 16, HEAD), BF16),
            pltpu.VMEM((cols - 1, HALF + 16, HEAD), BF16),
            pltpu.VMEM((HALF + 16, HEAD), BF16),
            pltpu.VMEM((heads, HALF + 16, HEAD), BF16),
            pltpu.SemaphoreType.DMA,
            pltpu.SemaphoreType.DMA,
            pltpu.SemaphoreType.DMA((16,)),
            pltpu.SemaphoreType.DMA((6, chunks)),
            pltpu.SemaphoreType.DMA((6, chunks)),
            pltpu.SemaphoreType.DMA((heads,)),
            pltpu.SemaphoreType.DMA((cols - 1,)),
            pltpu.SemaphoreType.DMA((cols,)),
            pltpu.SemaphoreType.DMA((heads,)),
            pltpu.SemaphoreType.REGULAR((4,)),
        ],
        compiler_params=pltpu.CompilerParams(
            collective_id=0, has_side_effects=True, vmem_limit_bytes=50 * 2**20
        ),
    )(*(pltpu.with_memory_space_constraint(value, pltpu.HBM) for value in (inputs, query_grads, momentum)))
    return pl.pallas_call(
        write_out,
        out_shape=(jax.ShapeDtypeStruct((rows, HEAD), F32),) * 2,
        in_specs=[pl.BlockSpec(memory_space=pltpu.VMEM)] * 2,
        out_specs=(pl.BlockSpec(memory_space=pltpu.HBM),) * 2,
        scratch_shapes=[pltpu.SemaphoreType.DMA, pltpu.SemaphoreType.DMA],
        compiler_params=pltpu.CompilerParams(vmem_limit_bytes=2**20),
    )(*done)


def solution(mesh):
    placed = (P("dp", "cols"), P("dp", None), P("dp", "cols"))
    return jax.shard_map(
        functools.partial(shards, mesh.shape["cols"], 4),
        mesh=mesh,
        in_specs=placed,
        out_specs=(P("dp", "cols"), P("dp", "cols")),
        check_vma=False,
    )
```

```python
import functools
import math

import jax
import jax.numpy as jnp
from jax import lax
from jax.experimental import pallas as pl
from jax.experimental.pallas import tpu as pltpu
from jax.sharding import PartitionSpec as P

HEAD = 128
HALF = HEAD // 2
STEPS = 5
AHEAD = 3
MOMENTUM_DECAY = 0.95
NORM_EPS = 1e-07
C1 = 3.4445
C3 = -4.775
C5 = 2.0315
MESH = pl.DeviceIdType.MESH
F32 = jnp.float32
BF16 = jnp.bfloat16

GRAD_CODE = (0.125, 2.0**-6, 4)
GRAM_CODE = (8.0, 2.0**-12, 3)
ROOT_CODE = (0.0625, 2.0**-6, 4)
RELAY_A, RELAY_B, DIRECT_B, DIRECT_A, SUM_A, SUM_B = range(6)


def encode(value, code):
    a, s, doublings = code
    grown = jnp.abs(value) * (s / a) + s
    for _ in range(doublings):
        grown = grown * grown
    return jnp.where(value < 0.0, -grown, grown).astype(BF16)


def decode(sent, code):
    a, s, doublings = code
    wide = sent.astype(F32)
    grown = jnp.exp(jnp.log(jnp.abs(wide)) * (0.5**doublings))
    size = grown * (a / s) - a
    return jnp.where(wide < 0.0, -size, size)


def split(value):
    high = value.astype(BF16)
    low = (value - high.astype(F32)).astype(BF16)
    return high, low


def dot_nn(a, b):
    return lax.dot_general(a, b, (((1,), (0,)), ((), ())), preferred_element_type=F32)


def dot_nt(a, b):
    return lax.dot_general(a, b, (((1,), (1,)), ((), ())), preferred_element_type=F32)


def mul3(a, b):
    ah, al = a
    bh, bl = b
    return dot_nn(jnp.concatenate([ah, al, ah, al], axis=1), jnp.concatenate([bh, bh, bl, bl], axis=0))


def iotas(rows):
    return (
        lax.broadcasted_iota(jnp.int32, (rows, HEAD), 0),
        lax.broadcasted_iota(jnp.int32, (rows, HEAD), 1),
    )


def pack(matrix):
    row, lane = iotas(HALF)
    return jnp.where(lane > row, matrix[:HALF], pltpu.roll(matrix[HALF:], HALF, 1))


def unpack(packed):
    row, lane = iotas(HALF)
    top = jnp.where(lane > row, packed, 0.0)
    bottom = pltpu.roll(jnp.where(lane < row, packed, 0.0), HALF, 1)
    half = jnp.concatenate([top, bottom], axis=0)
    return half + half.T


def kernel(
    dims,
    x_hbm,
    q_hbm,
    m_hbm,
    nm_ref,
    up_ref,
    x_ref,
    xt_ref,
    q_ref,
    m_ref,
    own_ref,
    zsend,
    zrecv,
    gsend,
    grecv,
    fsend,
    frecv,
    x_sem,
    m_sem,
    q_sem,
    zsend_sem,
    zrecv_sem,
    gsend_sem,
    grecv_sem,
    fsend_sem,
    frecv_sem,
    round_sem,
):
    cols, heads, chunks, width = dims
    half_rows = chunks * width
    rows = 2 * half_rows
    per_chunk = width // HEAD
    half_heads = heads // 2
    side = math.isqrt(cols // 2)
    groups = 2
    wide = half_rows // groups
    per_group = chunks // groups

    z = lax.axis_index("dp")
    c = lax.axis_index("cols")
    right = lax.rem(z + 1, 4)
    left = lax.rem(z + 3, 4)
    opposite = lax.rem(z + 2, 4)

    own_head = c // 2
    is_owner = jnp.logical_and(own_head < heads, lax.rem(c, 2) == lax.rem(own_head, 2))

    row, lane = iotas(HEAD)
    identity = jnp.where(row == lane, 1.0, 0.0)
    which = iotas(16)[0]

    def owner_of(head):
        return 2 * head + lax.rem(head, 2)

    x_copy = pltpu.make_async_copy(x_hbm, x_ref, x_sem)
    x_copy.start()

    def q_copy(slot, target, half, g):
        start = pl.multiple_of(target * rows + half * half_rows + g * wide, wide)
        return pltpu.make_async_copy(q_hbm.at[:, pl.ds(start, wide)], q_ref.at[slot], q_sem.at[slot])

    blocks = [(opposite, 0, 0), (opposite, 1, 0), (opposite, 0, 1), (opposite, 1, 1)]
    blocks += [(right, 1, 0), (left, 0, 0), (z, 0, 0), (z, 1, 0), (z, 0, 1), (z, 1, 1)]
    blocks += [(right, 0, 0), (left, 1, 0), (right, 1, 1), (left, 0, 1), (right, 0, 1), (left, 1, 1)]
    direct_slots = (4, 12)
    own_slots = (6, 8)
    sum_slots = (10, 14)
    for slot in range(AHEAD):
        q_copy(slot, *blocks[slot]).start()
    m_copy = pltpu.make_async_copy(m_hbm, m_ref, m_sem)

    core = lax.rem(c, 2)
    along_y = lax.rem(c // 2, side)
    along_x = c // (2 * side)

    def device(dx, dy, dc):
        return (lax.rem(along_x + dx, side) * side + lax.rem(along_y + dy, side)) * 2 + lax.rem(core + dc, 2)

    row_peers = [device(1, 0, 0), device(side - 1, 0, 0)]
    column_peers = [device(0, 1, 0), device(0, side - 1, 0)]
    other_core = device(0, 0, 1)
    barrier = pltpu.get_barrier_semaphore()
    near = [{"dp": right}, {"dp": left}] + [{"cols": peer} for peer in row_peers + column_peers + [other_core]]
    for peer in near:
        pl.semaphore_signal(barrier, inc=1, device_id=peer, device_id_type=MESH)

    rounds = (row_peers, column_peers, column_peers, [other_core])

    def tell(index):
        for peer in rounds[index]:
            pl.semaphore_signal(round_sem.at[index], inc=1, device_id={"cols": peer}, device_id_type=MESH)

    def heard(index):
        pl.semaphore_wait(round_sem.at[index], len(rounds[index]))

    x_copy.wait()
    xt_ref[...] = x_ref[...].T

    def q_wait(slot):
        q_copy(slot, *blocks[slot]).wait()
        if slot + AHEAD < len(blocks):
            q_copy(slot + AHEAD, *blocks[slot + AHEAD]).start()
        if slot + AHEAD == len(blocks):
            m_copy.start()

    def product(slot):
        return dot_nn(xt_ref[...], q_ref[slot])

    def z_copy(message, k, target):
        return pltpu.make_async_remote_copy(
            src_ref=zsend.at[message, k],
            dst_ref=zrecv.at[message, k],
            send_sem=zsend_sem.at[message, k],
            recv_sem=zrecv_sem.at[message, k],
            device_id={"dp": target},
            device_id_type=MESH,
        )

    def z_store(message, g, value):
        for i in range(per_group):
            zsend[message, g * per_group + i] = encode(value[:, i * width : (i + 1) * width], GRAD_CODE)

    def z_start(message, g, target):
        for i in range(per_group):
            z_copy(message, g * per_group + i, target).start()

    def z_wait(message, k):
        z_copy(message, k, right).wait_recv()

    def z_value(message, k):
        return decode(zrecv[message, k], GRAD_CODE)

    for half in range(2):
        q_wait(half)
        message, target = ((RELAY_A, right), (RELAY_B, left))[half]
        for i in range(per_group):
            value = dot_nn(xt_ref[...], q_ref[half, :, i * width : (i + 1) * width])
            zsend[message, i] = encode(value, GRAD_CODE)
            if half + i == 0:
                pl.semaphore_wait(barrier, len(near))
            z_copy(message, i, target).start()
    tell(0)
    for g in range(1, groups):
        q_wait(2 * g)
        z_store(RELAY_A, g, product(2 * g))
        z_start(RELAY_A, g, right)
        q_wait(2 * g + 1)
        z_store(RELAY_B, g, product(2 * g + 1))
        z_start(RELAY_B, g, left)

    def direct(g):
        slot = direct_slots[g]
        q_wait(slot)
        q_wait(slot + 1)
        z_store(DIRECT_B, g, product(slot))
        z_store(DIRECT_A, g, product(slot + 1))
        z_start(DIRECT_B, g, right)
        z_start(DIRECT_A, g, left)

    def sums(g):
        first = sum_slots[g]
        q_wait(first)
        q_wait(first + 1)
        for i in range(per_group):
            z_wait(RELAY_A, g * per_group + i)
            z_wait(RELAY_B, g * per_group + i)
        for message, arrived, slot in ((SUM_A, RELAY_A, first), (SUM_B, RELAY_B, first + 1)):
            mine = product(slot)
            for i in range(per_group):
                k = g * per_group + i
                value = mine[:, i * width : (i + 1) * width] + z_value(arrived, k)
                zsend[message, k] = encode(value, GRAD_CODE)
        z_start(SUM_A, g, right)
        z_start(SUM_B, g, left)

    heard(0)
    tell(1)
    direct(0)
    heard(1)
    tell(2)
    for g in range(groups):
        for half in range(2):
            q_wait(own_slots[g] + half)
        for half in range(2):
            own_ref[half, g] = product(own_slots[g] + half)
    heard(2)
    tell(3)
    sums(0)
    direct(1)
    m_copy.wait()
    heard(3)

    def g_copy(head):
        owner = owner_of(head)
        dx = lax.rem(along_x - owner // (2 * side) + side, side)
        dy = lax.rem(along_y - lax.rem(owner // 2, side) + side, side)
        dc = lax.rem(core + owner, 2)
        slot = jnp.maximum((dx * side + dy) * 2 + dc - 1, 0)
        return pltpu.make_async_remote_copy(
            src_ref=gsend.at[head],
            dst_ref=grecv.at[slot],
            send_sem=gsend_sem.at[head],
            recv_sem=grecv_sem.at[slot],
            device_id={"cols": owner},
            device_id_type=MESH,
        )

    def finish(k, carry):
        g = k // per_group
        inside = pl.multiple_of(lax.rem(k, per_group) * width, width)
        for message in (DIRECT_A, SUM_A, DIRECT_B, SUM_B):
            z_wait(message, k)
        done = []
        for half, (first, second) in enumerate(((DIRECT_A, SUM_A), (DIRECT_B, SUM_B))):
            total = own_ref[half, g, :, pl.ds(inside, width)] + (z_value(first, k) + z_value(second, k))
            for j in range(per_chunk):
                head = half * half_heads + k * per_chunk + j
                start = pl.multiple_of(head * HEAD, HEAD)
                block = m_ref[pl.ds(start, HEAD), :] * MOMENTUM_DECAY + total[:, j * HEAD : (j + 1) * HEAD].T
                nm_ref[pl.ds(start, HEAD), :] = block
                high, low = split(block)
                gram = dot_nt(
                    jnp.concatenate([high, low, high, low], axis=1), jnp.concatenate([high, high, low, low], axis=1)
                )
                diagonal = jnp.sum(gram * identity, axis=0, keepdims=True)
                gsend[head, pl.ds(0, HALF), :] = encode(pack(gram), GRAM_CODE)
                gsend[head, pl.ds(HALF, 16), :] = encode(jnp.broadcast_to(diagonal, (16, HEAD)), GRAM_CODE)
                done.append(head)
        for head in done:

            @pl.when(c != owner_of(head))
            def _():
                g_copy(head).start()

        return carry

    finish(0, 0)
    sums(1)
    lax.fori_loop(1, chunks, finish, 0)

    others = sorted(
        ((dx, dy, dc) for dx in range(side) for dy in range(side) for dc in range(2) if dx + dy + dc),
        key=lambda d: (min(d[0], side - d[0]) + min(d[1], side - d[1]), d[2]),
    )

    def f_copy(step):
        return pltpu.make_async_remote_copy(
            src_ref=fsend,
            dst_ref=frecv.at[own_head],
            send_sem=fsend_sem.at[step],
            recv_sem=frecv_sem.at[own_head],
            device_id={"cols": device(*others[step])},
            device_id_type=MESH,
        )

    @pl.when(is_owner)
    def _():
        def arrived(slot):
            pltpu.make_async_remote_copy(
                src_ref=gsend.at[0],
                dst_ref=grecv.at[slot],
                send_sem=gsend_sem.at[0],
                recv_sem=grecv_sem.at[slot],
                device_id={"cols": lax.rem(c + 1, cols)},
                device_id_type=MESH,
            ).wait_recv()

        slots = [(dx * side + dy) * 2 + dc - 1 for dx, dy, dc in others]
        total = decode(gsend[own_head], GRAM_CODE)
        for first in range(0, cols - 1, 4):
            for slot in slots[first : first + 4]:
                arrived(slot)
            for slot in slots[first : first + 4]:
                total += decode(grecv[slot], GRAM_CODE)
        diagonal = total[HALF : HALF + 1]
        gram = unpack(total[:HALF]) + identity * diagonal
        norm = jnp.sqrt(jnp.sum(diagonal, axis=1, keepdims=True)) + NORM_EPS
        current = gram / (norm * norm)
        factor = None
        for sweep in range(STEPS):
            parts = split(current)
            square = mul3(parts, parts)
            poly = C1 * identity + C3 * current + C5 * square
            poly_parts = split(poly)
            factor = poly if factor is None else mul3(poly_parts, split(factor))
            if sweep + 1 < STEPS:
                inner = mul3(parts, poly_parts)
                current = mul3(poly_parts, split(inner))
        diagonal = jnp.sum(factor * identity, axis=0, keepdims=True)
        mean = jnp.sum(diagonal, axis=1, keepdims=True) * (1.0 / HEAD)
        fsend[pl.ds(0, HALF), :] = encode(pack(factor), ROOT_CODE)
        pieces = jnp.broadcast_to(encode(diagonal - mean, ROOT_CODE).astype(F32), (16, HEAD))
        for first, rest in ((1, norm), (4, mean)):
            rest = jnp.broadcast_to(rest, (16, HEAD))
            for piece in range(3):
                part = rest.astype(BF16).astype(F32)
                pieces = jnp.where(which == first + piece, part, pieces)
                rest = rest - part
        fsend[pl.ds(HALF, 16), :] = pieces.astype(BF16)

        for step in reversed(range(cols - 1)):
            f_copy(step).start()
        frecv[own_head] = fsend[...]

    def apply(k, carry):
        members = [half * half_heads + k * per_chunk + j for half in range(2) for j in range(per_chunk)]
        for head in members:

            @pl.when(c != owner_of(head))
            def _():
                pltpu.make_async_remote_copy(
                    src_ref=fsend,
                    dst_ref=frecv.at[head],
                    send_sem=fsend_sem.at[0],
                    recv_sem=frecv_sem.at[head],
                    device_id={"cols": lax.rem(c + 1, cols)},
                    device_id_type=MESH,
                ).wait_recv()

        for head in members:
            pieces = frecv[head, pl.ds(HALF, 16), :].astype(F32)
            norm = pieces[1:2, :] + (pieces[2:3, :] + pieces[3:4, :])
            mean = pieces[4:5, :] + (pieces[5:6, :] + pieces[6:7, :])
            diagonal = decode(pieces[0:8, :], ROOT_CODE)[0:1] + mean
            factor = unpack(decode(frecv[head, pl.ds(0, HALF), :], ROOT_CODE)) + identity * diagonal
            start = pl.multiple_of(head * HEAD, HEAD)
            block = nm_ref[pl.ds(start, HEAD), :]
            scale = math.sqrt(cols * HEAD) / norm
            up_ref[pl.ds(start, HEAD), :] = mul3(split(factor), split(block)) * scale
        return carry

    def z_drain(k, carry):
        for message in range(6):
            z_copy(message, k, right).wait_send()
        return carry

    lax.fori_loop(0, chunks, z_drain, 0)

    def g_drain(head, carry):
        @pl.when(c != owner_of(head))
        def _():
            g_copy(head).wait_send()

        return carry

    lax.fori_loop(0, heads, g_drain, 0)
    lax.fori_loop(0, chunks - 1, apply, 0)

    @pl.when(is_owner)
    def _():
        for step in range(cols - 1):
            f_copy(step).wait_send()

    apply(chunks - 1, 0)


def write_out(nm_ref, up_ref, nm_hbm, up_hbm, nm_sem, up_sem):
    copies = [pltpu.make_async_copy(nm_ref, nm_hbm, nm_sem), pltpu.make_async_copy(up_ref, up_hbm, up_sem)]
    for copy in copies:
        copy.start()
    for copy in copies:
        copy.wait()


def shards(cols, chunks, inputs, query_grads, momentum):
    rows = momentum.shape[0]
    heads = rows // HEAD
    width = rows // (2 * chunks)
    wide = rows // 4
    tokens = inputs.shape[0]
    dims = (cols, heads, chunks, width)
    out = pltpu.VMEM((rows, HEAD), F32)
    done = pl.pallas_call(
        functools.partial(kernel, dims),
        out_shape=(out, out),
        in_specs=[pl.BlockSpec(memory_space=pltpu.HBM)] * 3,
        out_specs=(pl.BlockSpec(memory_space=pltpu.VMEM),) * 2,
        scratch_shapes=[
            pltpu.VMEM((tokens, HEAD), BF16),
            pltpu.VMEM((HEAD, tokens), BF16),
            pltpu.VMEM((16, tokens, wide), BF16),
            pltpu.VMEM((rows, HEAD), F32),
            pltpu.VMEM((2, 2, HEAD, wide), F32),
            pltpu.VMEM((6, chunks, HEAD, width), BF16),
            pltpu.VMEM((6, chunks, HEAD, width), BF16),
            pltpu.VMEM((heads, HALF + 16, HEAD), BF16),
            pltpu.VMEM((cols - 1, HALF + 16, HEAD), BF16),
            pltpu.VMEM((HALF + 16, HEAD), BF16),
            pltpu.VMEM((heads, HALF + 16, HEAD), BF16),
            pltpu.SemaphoreType.DMA,
            pltpu.SemaphoreType.DMA,
            pltpu.SemaphoreType.DMA((16,)),
            pltpu.SemaphoreType.DMA((6, chunks)),
            pltpu.SemaphoreType.DMA((6, chunks)),
            pltpu.SemaphoreType.DMA((heads,)),
            pltpu.SemaphoreType.DMA((cols - 1,)),
            pltpu.SemaphoreType.DMA((cols,)),
            pltpu.SemaphoreType.DMA((heads,)),
            pltpu.SemaphoreType.REGULAR((4,)),
        ],
        compiler_params=pltpu.CompilerParams(
            collective_id=0, has_side_effects=True, vmem_limit_bytes=50 * 2**20
        ),
    )(*(pltpu.with_memory_space_constraint(value, pltpu.HBM) for value in (inputs, query_grads, momentum)))
    return pl.pallas_call(
        write_out,
        out_shape=(jax.ShapeDtypeStruct((rows, HEAD), F32),) * 2,
        in_specs=[pl.BlockSpec(memory_space=pltpu.VMEM)] * 2,
        out_specs=(pl.BlockSpec(memory_space=pltpu.HBM),) * 2,
        scratch_shapes=[pltpu.SemaphoreType.DMA, pltpu.SemaphoreType.DMA],
        compiler_params=pltpu.CompilerParams(vmem_limit_bytes=2**20),
    )(*done)


def solution(mesh):
    placed = (P("dp", "cols"), P("dp", None), P("dp", "cols"))
    return jax.shard_map(
        functools.partial(shards, mesh.shape["cols"], 4),
        mesh=mesh,
        in_specs=placed,
        out_specs=(P("dp", "cols"), P("dp", "cols")),
        check_vma=False,
    )
```
